256 devices in a mesh: rows: 64 (over z, y, core), cols: 4 (over x).
Axes of the slice: x: 4, y: 4, z: 8, core: 2. Of those that a mesh axis runs over, the one named last changes fastest.
Arguments:
- feats_t: bfloat16 [128, 131072], P('cols', 'rows'), may hold values from -6 to 6
- adj_index: int32 [1024, 16], replicated, may hold values from 0 to 1023, as said below
- adj_weight: bfloat16 [1024, 16, 128, 128], P('rows'), as said below
- weight: bfloat16 [128, 256], replicated, may hold values from -0.5 to 0.5
- cotangent_t: bfloat16 [256, 131072], P('cols', 'rows'), may hold values from -6 to 6
Outputs:
- output_t: bfloat16 [256, 131072], P('cols', 'rows')
- weight_grad: float32 [128, 256], P('cols')
- feat_grad: float32 [128, 131072], P('cols', 'rows')
The draws below stay inside these ranges and needn't reach their ends.
Inputs may be any that keep to these rules, and one draw needn't show every extreme that they name: `adj_index`: slot 0 of row block i names block i itself. Blocks are grouped 16 to a device in order. Slot 1 names a block of the next device (device index plus one, cyclically). The row blocks of one device name at most 4 distinct blocks of any other device, and exactly 4 of the next one. A block may stand in several slots of one row block. `adj_weight`: Nonnegative; about one entry in eight is nonzero.
All inputs are finite; a program needn't handle non-finite values.
Results may differ from the reference program's by a relative error of at most 0.0054.
Values may be sent and summed in bfloat16 or wider, within the bound.
A program may use at most 128 MiB of HBM per device.

```python
import jax
import jax.numpy as jnp
from jax import lax

F_IN = 128
UNITS = 256
TILE = 128
KB = 16
BLK_DEV = 16
CAP = 4
NB = 1024
NODES = 131072


def draw_adj_index(key, part):
    row_devs = NB // BLK_DEV
    key_sub, key_src, key_pick = jax.random.split(jax.random.fold_in(key, 11), 3)
    scores = jax.random.randint(key_sub, (row_devs, row_devs, BLK_DEV), 0, 2 ** 20) * BLK_DEV + jnp.arange(BLK_DEV, dtype=jnp.int32)
    subset = lax.top_k(scores, CAP)[1].astype(jnp.int32)
    blocks = jnp.arange(NB, dtype=jnp.int32)
    owner = blocks // BLK_DEV
    within = blocks % BLK_DEV
    after = (owner + 1) % row_devs
    first = after * BLK_DEV + subset[owner, after, within % CAP]
    offsets = jax.random.randint(key_src, (NB, KB - 2), 1, row_devs)
    source = (owner[:, None] + offsets) % row_devs
    choose = jax.random.randint(key_pick, (NB, KB - 2), 0, CAP)
    others = source * BLK_DEV + subset[owner[:, None], source, choose]
    return jnp.concatenate([blocks[:, None], first[:, None], others], axis=1).astype(jnp.int32)


def draw_adj_weight(key, part):
    key_mask, key_val = jax.random.split(jax.random.fold_in(key, 23))
    shape = (NB, KB, TILE, TILE)
    present = (jax.random.uniform(key_mask, shape) < 0.125).astype(jnp.float32)
    values = jax.random.uniform(key_val, shape, minval=0.5, maxval=1.5)
    norm = 1.0 / jnp.sqrt(jnp.float32(KB * TILE) / 8.0)
    return (present * values * norm).astype(jnp.bfloat16)


def level_of(own_key, dims, pieces, low, high):
    gain, own = 1.0, jax.random.fold_in(own_key, 6)
    for dim, parts in pieces:
        draws = jnp.exp(jax.random.uniform(jax.random.fold_in(own, dim), (parts,), jnp.float32, low / len(pieces), high / len(pieces)))
        gain = gain * jnp.repeat(draws, dims[dim] // parts).reshape([-1 if axis == dim else 1 for axis in range(len(dims))])
    return gain


def gaussian(stream_key, shape, scale, bound, cuts=(), held_as=jnp.bfloat16):
    gain = level_of(stream_key, shape, cuts, -0.22, 0.18) if cuts else 1.0
    drawn = jax.random.normal(stream_key, shape, jnp.float32) * scale * gain
    return jnp.minimum(jnp.maximum(drawn, -bound), bound).astype(held_as)


def setup_inputs(seed: int = 0) -> dict:
    arg_keys = jax.random.split(jax.random.key(seed), 6)
    feats_t = gaussian(arg_keys[0], (F_IN, NODES), 1.0, 6.0, ((0, 4), (1, 64)))
    adj_index = draw_adj_index(jax.random.fold_in(arg_keys[5], 71), 0)
    adj_weight = draw_adj_weight(jax.random.fold_in(arg_keys[5], 71), 0)
    weight = gaussian(arg_keys[3], (F_IN, UNITS), F_IN ** -0.5, 0.5)
    cotangent_t = gaussian(arg_keys[4], (UNITS, NODES), 1.0, 6.0, ((0, 4), (1, 64)))
    return {"feats_t": feats_t, "adj_index": adj_index, "adj_weight": adj_weight, "weight": weight, "cotangent_t": cotangent_t}


def reference(feats_t, adj_index, adj_weight, weight, cotangent_t):
    feat_blocks = feats_t.reshape(F_IN, NB, TILE)

    def aggregate(block_id):
        picked = jnp.take(feat_blocks, adj_index[block_id], axis=1).astype(jnp.float32)
        return jnp.einsum('fkj,kij->fi', picked, adj_weight[block_id].astype(jnp.float32), precision=lax.Precision.HIGHEST)
    summed = lax.map(aggregate, jnp.arange(NB))
    aggregated = summed.transpose(1, 0, 2).reshape(F_IN, NODES).astype(jnp.bfloat16)
    pre_act = jnp.dot(weight.T, aggregated, preferred_element_type=jnp.float32)
    output_t = jax.nn.silu(pre_act).astype(jnp.bfloat16)
    sigm = jax.nn.sigmoid(pre_act)
    pre_grad = (cotangent_t.astype(jnp.float32) * sigm * (1.0 + pre_act * (1.0 - sigm))).astype(jnp.bfloat16)
    weight_grad = jnp.dot(aggregated, pre_grad.T, preferred_element_type=jnp.float32) / jnp.sqrt(jnp.float32(NODES))
    agg_grad = jnp.dot(weight, pre_grad, preferred_element_type=jnp.float32).astype(jnp.bfloat16)
    grad_blocks = agg_grad.reshape(F_IN, NB, TILE)

    def spread(accum, block_id):
        terms = jnp.einsum('fi,kij->kfj', grad_blocks[:, block_id].astype(jnp.float32), adj_weight[block_id].astype(jnp.float32), precision=lax.Precision.HIGHEST)
        return (accum.at[adj_index[block_id]].add(terms), None)
    accum, _ = lax.scan(spread, jnp.zeros((NB, F_IN, TILE), jnp.float32), jnp.arange(NB))
    feat_grad = accum.transpose(1, 0, 2).reshape(F_IN, NODES)
    return (output_t, weight_grad, feat_grad)
```

```python
import math

import jax
import jax.numpy as jnp
from jax import lax
from jax.experimental import pallas as pl
from jax.experimental.pallas import tpu as pltpu
from jax.sharding import PartitionSpec as P

MESH = pl.DeviceIdType.MESH
NZ, NY, NC, NX = 8, 4, 2, 4
BLK, KB, TILE, CAP, FR, UR = 16, 16, 128, 4, 32, 64
NODES_DEV = BLK * TILE
CH = 4
CN = NODES_DEV // CH
OWN = 64 * CAP
ZERO = BLK * KB
FWD_ORDER = (0, 7, 1, 6, 2, 5, 3, 4)
BWD_ORDER = (4, 3, 5, 2, 6, 1, 7, 0)
F32, BF16 = jnp.float32, jnp.bfloat16
NT = (((1,), (1,)), ((), ()))


def tables(adj_index, r, z, y, c):
    i32 = jnp.int32
    rows8 = lax.dynamic_slice_in_dim(adj_index, z * 8 * BLK, 8 * BLK, 0).reshape(8, 1, BLK * KB)
    t = jnp.arange(NZ * BLK, dtype=i32)
    target = (t // BLK) * (8 * BLK) + y * (2 * BLK) + c * BLK + t % BLK
    named = jnp.any(rows8 == target[None, :, None], axis=2)
    named = named.reshape(8, NZ, BLK)
    b = jnp.arange(BLK, dtype=i32)
    rank = jnp.sum(jnp.where((b[None, :] < b[:, None])[None, None], named[:, :, None, :], False), axis=3, dtype=i32)
    k = jnp.arange(CAP, dtype=i32)
    hit = named[:, :, None, :] & (rank[:, :, None, :] == k[None, None, :, None])
    send = jnp.sum(jnp.where(hit, b[None, None, None, :], 0), axis=3, dtype=i32)
    d = jnp.arange(8, dtype=i32)
    own_pair = (d[:, None, None] == y * 2 + c) & (jnp.arange(NZ, dtype=i32)[None, :, None] == z)
    take = jnp.where(named & ~own_pair, d[:, None, None] * CAP + jnp.minimum(rank, CAP - 1), 8 * CAP)
    take = take.transpose(1, 2, 0)
    own = lax.dynamic_slice_in_dim(adj_index, r * BLK, BLK, 0).reshape(BLK * KB)
    j = jnp.arange(64 * BLK, dtype=i32)
    present = jnp.any(own[None, :] == j[:, None], axis=1)
    before = present[None, :] & (j[None, :] // BLK == own[:, None] // BLK) & (j[None, :] < own[:, None])
    slot = (own // BLK) * CAP + jnp.sum(before, axis=1, dtype=i32)
    slot = jnp.where(own // BLK == r, OWN + own % BLK, slot)
    e = jnp.arange(BLK * KB, dtype=i32)
    pos = jnp.sum((slot[None, :] < slot[:, None]) | ((slot[None, :] == slot[:, None]) & (e[None, :] < e[:, None])), axis=1, dtype=i32)
    at = pos[None, :] == e[:, None]
    order = jnp.sum(jnp.where(at, e[None, :], 0), axis=1, dtype=i32)
    sslot = jnp.sum(jnp.where(at, slot[None, :], 0), axis=1, dtype=i32)
    keep = jnp.concatenate([jnp.zeros((1,), F32), (sslot[1:] == sslot[:-1]).astype(F32)])
    s = jnp.arange(OWN + BLK, dtype=i32)
    count = jnp.sum(slot[None, :] <= s[:, None], axis=1, dtype=i32)
    less = jnp.sum(slot[None, :] < s[:, None], axis=1, dtype=i32)
    last = jnp.where(count > less, count - 1, ZERO)
    return send.reshape(-1), slot, order, keep, last, take.reshape(-1)


def kernel(
    send_t, slot_t, order_t, keep_t, last_t, take_t, feats, cot, w_rows, w_cols, adj_hbm,
    out, wg_out, fg_out,
    adj, zb, pk, panel, fwp, fwm, xg, gsend, grecv, gown, grad, pref, pk2, rb, fw2p, fw2m, zs_buf, zrp, zrm,
    wpart, wsib, wy, wz, wx, wt,
    adj_sem, zss, zrs, yss, yrs, xss, xrs, gss, grs, yss2, yrs2, zss2, zrs2, wss, wrs,
):
    r = lax.axis_index("rows")
    x = lax.axis_index("cols")
    z, y, c = r // 8, (r // 2) % 4, r % 2
    me = y * 2 + c

    def dev(dz=0, dy=0, dc=0, dx=0):
        row = ((z + dz) % NZ) * 8 + ((y + dy) % NY) * 2 + (c + dc) % 2
        return {"rows": row, "cols": (x + dx) % NX}

    def rcopy(src, dst, ss, rs, **off):
        return pltpu.make_async_remote_copy(
            src_ref=src, dst_ref=dst, send_sem=ss, recv_sem=rs, device_id=dev(**off), device_id_type=MESH
        )

    adj_copy = pltpu.make_async_copy(adj_hbm, adj, adj_sem)
    adj_copy.start()
    peers = [dict(dz=d) for d in range(1, 8)]
    peers += [dict(dy=a, dc=b) for a in range(4) for b in range(2) if (a or b) and (a, b) != (2, 1)]
    peers += [dict(dx=a, dc=b) for a in range(1, 4) for b in range(2)]
    barrier = pltpu.get_barrier_semaphore()
    for off in peers:
        pl.semaphore_signal(barrier, inc=1, device_id=dev(**off), device_id_type=MESH)

    for b in range(BLK):
        blk = feats[:, b * TILE:(b + 1) * TILE]
        zb[0][b] = blk
        panel[OWN + b] = blk
    pl.semaphore_wait(barrier, len(peers))

    pending = []

    half = BLK // 2
    whole = pl.ds(0, BLK)
    zcopies = {}

    def zsend(src, dst, direction, blocks):
        cp = rcopy(zb[src].at[blocks], zb[dst].at[blocks], zss.at[dst + 8 * (direction > 0)], zrs.at[dst + 8 * (direction > 0)], dz=direction)
        cp.start()
        zcopies.setdefault(dst, []).append(cp)
        pending.append(cp)

    def pack(dz, src, put, self_put):
        zs = (z + dz) % NZ

        def one(i, carry):
            dd = ((y + i // 2) % NY) * 2 + (c + i % 2) % 2
            src(i, dd, zs)
            return carry

        lax.fori_loop(0 if self_put else 1, 8, one, 0)

    def ysends(dz, packs, dst_of, fp, fm, ss, rs, copies):
        list_ = []
        for n, (dy, dc) in enumerate(((1, 0), (1, 1), (3, 0), (3, 1), (0, 1))):
            cp = rcopy(packs.at[dz, dy * 2 + dc], dst_of(dz, y), ss.at[dz * 9 + n], rs.at[dz * 9 + n], dy=dy, dc=dc)
            list_.append(cp)
        a = rcopy(packs.at[dz, 4], fp.at[dz], ss.at[dz * 9 + 7], rs.at[dz * 9 + 7], dy=1)
        b = rcopy(packs.at[dz, 5], fm.at[dz], ss.at[dz * 9 + 8], rs.at[dz * 9 + 8], dy=3)
        for cp in (a, b, *list_):
            cp.start()
            pending.append(cp)
        copies[dz] = (list_, a, b)

    def forwards(dz, dst_of, fp, fm, ss, rs, copies):
        list_, a, b = copies[dz]
        a.wait_recv()
        f = rcopy(fp.at[dz], dst_of(dz, (y + 3) % NY), ss.at[dz * 9 + 5], rs.at[dz * 9 + 5], dy=1, dc=0)
        f.start()
        b.wait_recv()
        g = rcopy(fm.at[dz], dst_of(dz, (y + 1) % NY), ss.at[dz * 9 + 6], rs.at[dz * 9 + 6], dy=3, dc=1)
        g.start()
        pending.extend((f, g))
        list_ += [f, g]

    def panel_of(dz, yy):
        return panel.at[pl.ds((((z + dz) % NZ) * 8 + yy * 2 + c) * CAP, CAP)]

    ycopies = {}
    zsend(0, 7, 1, whole)
    zsend(0, 1, -1, whole)
    previous = None
    for dz in FWD_ORDER:
        if dz:
            for cp in zcopies[dz]:
                cp.wait_recv()
            if dz in (7, 6):
                zsend(dz, dz - 1, 1, whole)
            elif dz == 5:
                zsend(5, 4, 1, pl.ds(0, half))
            elif dz in (1, 2):
                zsend(dz, dz + 1, -1, whole)
            elif dz == 3:
                zsend(3, 4, -1, pl.ds(half, half))

        def message(i, dd, zs, dz=dz):
            for k in range(CAP):
                pk[dz, i, k] = zb[dz][send_t[(dd * NZ + zs) * CAP + k]]

        pack(dz, message, None, False)
        if dz:
            zs = (z + dz) % NZ
            for k in range(CAP):
                panel[(zs * 8 + me) * CAP + k] = zb[dz][send_t[(me * NZ + zs) * CAP + k]]
        ysends(dz, pk, panel_of, fwp, fwm, yss, yrs, ycopies)
        if previous is not None:
            forwards(previous, panel_of, fwp, fwm, yss, yrs, ycopies)
        previous = dz
    forwards(previous, panel_of, fwp, fwm, yss, yrs, ycopies)
    adj_copy.wait()
    for dz in FWD_ORDER:
        for cp in ycopies[dz][0]:
            cp.wait_recv()

    xcopies = {}
    for q in range(CH):

        def block(n, carry, q=q):
            i = q * (BLK // CH) + n
            acc = jnp.zeros((FR, TILE), F32)
            for k in range(0, KB, 2):
                left = jnp.concatenate([panel[slot_t[i * KB + k]], panel[slot_t[i * KB + k + 1]]], axis=1)
                right = jnp.concatenate([adj[i * KB + k], adj[i * KB + k + 1]], axis=1)
                acc += lax.dot_general(left, right, NT, preferred_element_type=F32)
            xg[0, q, :, pl.ds(pl.multiple_of(n * TILE, TILE), TILE)] = acc.astype(BF16)
            return carry

        lax.fori_loop(0, BLK // CH, block, 0)
        for dx in (2, 1, 3):
            cp = rcopy(xg.at[0, q], xg.at[4 - dx, q], xss.at[q * 4 + dx], xrs.at[q * 4 + dx], dx=dx)
            cp.start()
            pending.append(cp)
            xcopies[q, dx] = cp

    gcopies = {}
    for q in range(CH):
        cols = pl.ds(q * CN, CN)
        for dx in (1, 3, 2):
            xcopies[q, dx].wait_recv()
        agg = xg[:, q].reshape(NX * FR, CN)
        pre = jnp.dot(w_cols[...], agg, preferred_element_type=F32)
        sig = jax.nn.sigmoid(pre)
        out[:, cols] = (pre * sig).astype(BF16)
        pg = (cot[:, cols].astype(F32) * sig * (1.0 + pre * (1.0 - sig))).astype(BF16)
        part = jnp.dot(w_rows[...], pg, preferred_element_type=F32)
        gown[q] = part[0:FR]
        for dx in (2, 1, 3):
            gsend[dx, q] = part[dx * FR:(dx + 1) * FR].astype(BF16)
            cp = rcopy(gsend.at[dx, q], grecv.at[4 - dx, q], gss.at[q * 4 + dx], grs.at[q * 4 + dx], dx=dx)
            cp.start()
            pending.append(cp)
            gcopies[q, dx] = cp
        wg = lax.dot_general(pg, agg, NT, preferred_element_type=F32)
        if q == 0:
            wpart[...] = wg
        else:
            wpart[...] += wg

    hu = UR // 2
    w1 = rcopy(wpart.at[pl.ds(pl.multiple_of((1 - c) * hu, 8), hu)], wsib, wss.at[0], wrs.at[0], dc=1)
    w1.start()
    pending.append(w1)

    for q in range(CH):
        for dx in (1, 3, 2):
            gcopies[q, dx].wait_recv()
        g = gown[q] + grecv[1, q].astype(F32) + grecv[2, q].astype(F32) + grecv[3, q].astype(F32)
        g = g.astype(BF16)
        for n in range(BLK // CH):
            grad[q * (BLK // CH) + n] = g[:, n * TILE:(n + 1) * TILE]

    w1.wait_recv()
    wy[y] = wpart[pl.ds(pl.multiple_of(c * hu, 8), hu)] + wsib[...]
    w2 = []
    for dy in (1, 2, 3):
        cp = rcopy(wy.at[y], wy.at[y], wss.at[dy], wrs.at[dy], dy=dy)
        cp.start()
        pending.append(cp)
        w2.append(cp)

    def entry(p, carry):
        e = order_t[p]
        pref[p] = jnp.dot(grad[lax.shift_right_logical(e, 4)], adj[e], preferred_element_type=F32)
        return carry

    lax.fori_loop(0, BLK * KB, entry, 0, unroll=8)

    def running(p, acc):
        acc = pref[p] + keep_t[p] * acc
        pref[p] = acc
        return acc

    lax.fori_loop(0, BLK * KB, running, jnp.zeros((FR, TILE), F32), unroll=8)
    pref[ZERO] = jnp.zeros((FR, TILE), F32)

    for cp in w2:
        cp.wait_recv()
    wz[z] = (wy[0] + wy[1]) + (wy[2] + wy[3])
    w3 = []
    for dz in range(1, NZ):
        cp = rcopy(wz.at[z], wz.at[z], wss.at[3 + dz], wrs.at[3 + dz], dz=dz)
        cp.start()
        pending.append(cp)
        w3.append(cp)

    ycopies2 = {}

    def rb_of(dz, yy):
        return rb[dz].at[pl.ds((yy * 2 + c) * CAP, CAP)]

    for dz in range(NZ):
        rb[dz][8 * CAP] = jnp.zeros((FR, TILE), BF16)
    previous = None
    for dz in BWD_ORDER:

        def term(i, dd, zs, dz=dz):
            for k in range(CAP):
                pk2[dz, i, k] = pref[last_t[(zs * 8 + dd) * CAP + k]].astype(BF16)

        pack(dz, term, None, False)
        zs = (z + dz) % NZ
        for k in range(CAP):
            if dz:
                rb[dz][me * CAP + k] = pref[last_t[(zs * 8 + me) * CAP + k]].astype(BF16)
            else:
                rb[dz][me * CAP + k] = jnp.zeros((FR, TILE), BF16)
        ysends(dz, pk2, rb_of, fw2p, fw2m, yss2, yrs2, ycopies2)
        if previous is not None:
            forwards(previous, rb_of, fw2p, fw2m, yss2, yrs2, ycopies2)
        previous = dz
    forwards(previous, rb_of, fw2p, fw2m, yss2, yrs2, ycopies2)

    for cp in w3:
        cp.wait_recv()
    wx[0, c] = (((wz[0] + wz[1]) + (wz[2] + wz[3])) + ((wz[4] + wz[5]) + (wz[6] + wz[7]))) * (
        1.0 / math.sqrt(NODES_DEV * 64)
    )
    w4 = []
    for dx in range(4):
        for dc in range(2):
            if dx or dc:
                n = 11 + dx * 2 + dc
                cp = rcopy(wx.at[0, c], wx.at[(4 - dx) % 4, c], wss.at[n], wrs.at[n], dx=dx, dc=dc)
                cp.start()
                pending.append(cp)
                w4.append(cp)

    zin = {}
    for dz in BWD_ORDER:
        for cp in ycopies2[dz][0]:
            cp.wait_recv()
        for cp in zin.get(dz, ()):
            cp.wait_recv()
        zs = (z + dz) % NZ

        def total(b, carry, dz=dz, zs=zs):
            acc = jnp.zeros((FR, TILE), F32)
            for n in range(8):
                acc += rb[dz][take_t[(zs * BLK + b) * 8 + n]].astype(F32)
            if dz in (1, 2):
                acc += zrp[dz, b].astype(F32)
            if dz in (6, 7):
                acc += zrm[dz, b].astype(F32)
            if dz == 0:
                acc += zrp[0, b].astype(F32) + zrm[0, b].astype(F32) + pref[last_t[OWN + b]]
                fg_out[:, pl.ds(pl.multiple_of(b * TILE, TILE), TILE)] = acc
            else:
                zs_buf[dz, b] = acc.astype(BF16)
            return carry

        def total_more(b, carry, dz=dz, zs=zs):
            off = 0 if dz == 3 else half
            acc = (zrp if dz == 3 else zrm)[dz, off + b].astype(F32)
            for n in range(8):
                acc += rb[dz][take_t[(zs * BLK + off + b) * 8 + n]].astype(F32)
            zs_buf[dz, off + b] = acc.astype(BF16)
            return carry

        def total_less(b, carry, dz=dz, zs=zs):
            off = half if dz == 3 else 0
            acc = jnp.zeros((FR, TILE), F32)
            for n in range(8):
                acc += rb[dz][take_t[(zs * BLK + off + b) * 8 + n]].astype(F32)
            zs_buf[dz, off + b] = acc.astype(BF16)
            return carry

        if dz in (3, 5):
            lax.fori_loop(0, half, total_more, 0)
            lax.fori_loop(0, half, total_less, 0)
        else:
            lax.fori_loop(0, BLK, total, 0)

        def ring(direction, blocks):
            to = dz - direction if dz - direction != 8 else 0
            buf = zrp if direction > 0 else zrm
            n = dz + 8 * (direction > 0)
            cp = rcopy(zs_buf.at[dz, blocks], buf.at[to, blocks], zss2.at[n], zrs2.at[n], dz=direction)
            cp.start()
            pending.append(cp)
            zin.setdefault(to, []).append(cp)

        if dz == 4:
            ring(1, pl.ds(0, half))
            ring(-1, pl.ds(half, half))
        elif dz in (1, 2, 3):
            ring(1, whole)
        elif dz in (5, 6, 7):
            ring(-1, whole)

    for cp in w4:
        cp.wait_recv()
    for dx in range(4):
        for cc in range(2):
            f0 = ((4 - dx) % 4) * FR
            row = pl.multiple_of(((x + dx) % NX) * UR + cc * hu, 8)
            wt[pl.ds(row, hu), 0:FR] = wx[dx, cc][:, f0:f0 + FR]
    wg_out[...] = wt[...].T[0:FR]

    for cp in pending:
        cp.wait_send()


def body(feats_t, adj_index, adj_weight, weight, cotangent_t):
    r = lax.axis_index("rows")
    x = lax.axis_index("cols")
    z, y, c = r // 8, (r // 2) % 4, r % 2
    tabs = tables(adj_index, r, z, y, c)
    w = lax.dynamic_slice_in_dim(weight, x * UR, UR, 1)
    w_rows = lax.dynamic_slice_in_dim(jnp.concatenate([w, w], axis=0), x * FR, NX * FR, 0)
    w_cols = w_rows.T
    vmem = pl.BlockSpec(memory_space=pltpu.VMEM)
    smem = pl.BlockSpec(memory_space=pltpu.SMEM)
    dma = pltpu.SemaphoreType.DMA
    blk = (FR, TILE)
    V = pltpu.VMEM
    return pl.pallas_call(
        kernel,
        out_shape=(
            jax.ShapeDtypeStruct((UR, NODES_DEV), BF16),
            jax.ShapeDtypeStruct((FR, NX * UR), F32),
            jax.ShapeDtypeStruct((FR, NODES_DEV), F32),
        ),
        in_specs=[smem] * 6 + [vmem] * 4 + [pl.BlockSpec(memory_space=pl.ANY)],
        out_specs=(vmem, vmem, vmem),
        scratch_shapes=[
            V((BLK * KB, TILE, TILE), BF16),
            [V((BLK, *blk), BF16) for _ in range(NZ)],
            V((NZ, 8, CAP, *blk), BF16),
            V((OWN + BLK, *blk), BF16),
            V((NZ, CAP, *blk), BF16),
            V((NZ, CAP, *blk), BF16),
            V((NX, CH, FR, CN), BF16),
            V((NX, CH, FR, CN), BF16),
            V((NX, CH, FR, CN), BF16),
            V((CH, FR, CN), F32),
            V((BLK, *blk), BF16),
            V((BLK * KB + 1, *blk), F32),
            V((NZ, 8, CAP, *blk), BF16),
            [V((8 * CAP + 1, *blk), BF16) for _ in range(NZ)],
            V((NZ, CAP, *blk), BF16),
            V((NZ, CAP, *blk), BF16),
            V((NZ, BLK, *blk), BF16),
            V((NZ, BLK, *blk), BF16),
            V((NZ, BLK, *blk), BF16),
            V((UR, NX * FR), F32),
            V((UR // 2, NX * FR), F32),
            V((NY, UR // 2, NX * FR), F32),
            V((NZ, UR // 2, NX * FR), F32),
            V((NX, NC, UR // 2, NX * FR), F32),
            V((NX * UR, TILE), F32),
            dma,
            dma((16,)),
            dma((16,)),
            dma((9 * NZ,)),
            dma((9 * NZ,)),
            dma((16,)),
            dma((16,)),
            dma((16,)),
            dma((16,)),
            dma((9 * NZ,)),
            dma((9 * NZ,)),
            dma((16,)),
            dma((16,)),
            dma((19,)),
            dma((19,)),
        ],
        compiler_params=pltpu.CompilerParams(
            collective_id=0, has_side_effects=True, vmem_limit_bytes=56 * 2**20
        ),
        name="gcn_step",
    )(*tabs, feats_t, cotangent_t, w_rows, w_cols, adj_weight.reshape(BLK * KB, TILE, TILE))


def solution(mesh):
    return jax.shard_map(
        body,
        mesh=mesh,
        in_specs=(P("cols", "rows"), P(), P("rows", None, None, None), P(), P("cols", "rows")),
        out_specs=(P("cols", "rows"), P("cols", None), P("cols", "rows")),
        check_vma=False,
    )
```

```python
import math

import jax
import jax.numpy as jnp
from jax import lax
from jax.experimental import pallas as pl
from jax.experimental.pallas import tpu as pltpu
from jax.sharding import PartitionSpec as P

MESH = pl.DeviceIdType.MESH
NZ, NY, NC, NX = 8, 4, 2, 4
BLK, KB, TILE, CAP, FR, UR = 16, 16, 128, 4, 32, 64
NODES_DEV = BLK * TILE
CH = 4
CN = NODES_DEV // CH
OWN = 64 * CAP
ZERO = BLK * KB
FWD_ORDER = (0, 7, 1, 6, 2, 5, 3, 4)
BWD_ORDER = (4, 3, 5, 2, 6, 1, 7, 0)
FWIN, BWIN, LAG = 2, 2, 3
F32, BF16 = jnp.float32, jnp.bfloat16
NT = (((1,), (1,)), ((), ()))


def group_sum(v, lane):
    n = v.shape[1]
    for step in (1, 2, 4, 8):
        up = pltpu.roll(v, n - step, 1)
        down = pltpu.roll(v, step, 1)
        v = v + jnp.where((lane & step) == 0, up, down)
    return v


def group_rank(named, lane):
    rank = jnp.zeros_like(named)
    for step in range(1, BLK):
        rank = rank + jnp.where((lane & (BLK - 1)) >= step, pltpu.roll(named, step, 1), 0)
    return rank


def send_tables(rows8, send_v, take_v, y, z, c, me):
    lane = lax.broadcasted_iota(jnp.int32, (8 * BLK, TILE), 1)
    target = (lane >> 4) * (8 * BLK) + (lane & 15) + (y * 2 + c) * BLK
    hit = jnp.zeros((8 * BLK, TILE), jnp.int32)
    for k in range(KB):
        hit = jnp.where(rows8[:, k:k + 1] == target, 1, hit)
    named = jnp.max(hit.reshape(8, BLK, TILE), axis=1)
    lane = lax.broadcasted_iota(jnp.int32, (8, TILE), 1)
    rank = group_rank(named, lane)
    for k in range(CAP):
        send_v[k * 8:(k + 1) * 8] = group_sum(jnp.where((named > 0) & (rank == k), lane & 15, 0), lane)
    d = lax.broadcasted_iota(jnp.int32, (8, TILE), 0)
    use = (named > 0) & ((d != me) | ((lane >> 4) != z))
    take_v[...] = jnp.where(use, d * CAP + jnp.minimum(rank, CAP - 1), 8 * CAP)


def slot_tables(rows8, slot_v, prev_v, last_v, r, me):
    own = rows8[pl.ds(pl.multiple_of(me * BLK, BLK), BLK)]
    lane = lax.broadcasted_iota(jnp.int32, (BLK, 64 * BLK), 1)
    hit = jnp.zeros((BLK, 64 * BLK), jnp.int32)
    for k in range(KB):
        hit = jnp.where(own[:, k:k + 1] == lane, 1, hit)
    lane8 = lax.broadcasted_iota(jnp.int32, (8, 64 * BLK), 1)
    named = jnp.broadcast_to(jnp.max(hit, axis=0, keepdims=True), (8, 64 * BLK))
    value = (lane8 >> 4) * CAP + jnp.minimum(group_rank(named, lane8), CAP - 1)
    value = jnp.where((lane8 >> 4) == r, OWN + (lane8 & 15), value)
    value = jnp.concatenate([value, value], axis=0)
    small = lax.broadcasted_iota(jnp.int32, (BLK, TILE), 1)
    e_lane = lax.broadcasted_iota(jnp.int32, (BLK, BLK * KB), 1)
    row = lax.broadcasted_iota(jnp.int32, (BLK, BLK * KB), 0)
    t_lane = lax.broadcasted_iota(jnp.int32, (BLK, 3 * TILE), 1)
    t_row = lax.broadcasted_iota(jnp.int32, (BLK, 3 * TILE), 0)
    slots = jnp.zeros((BLK, TILE), jnp.int32)
    spread = jnp.zeros((BLK, BLK * KB), jnp.int32)
    last = jnp.full((BLK, 3 * TILE), -1, jnp.int32)
    columns = []
    for k in range(KB):
        col = jnp.max(jnp.where(own[:, k:k + 1] == lane, value, 0), axis=1, keepdims=True)
        columns.append(col)
        slots = jnp.where(small == k, col, slots)
        spread = jnp.where((e_lane & 15) == k, col, spread)
        last = jnp.maximum(last, jnp.where(col == t_lane, t_row * KB + k, -1))
    slot_v[...] = slots
    by_lane = jnp.max(jnp.where((e_lane >> 4) == row, spread, 0), axis=0, keepdims=True)
    prev = jnp.zeros((BLK, TILE), jnp.int32)
    for k in range(KB):
        same = (columns[k] == by_lane) & (e_lane < row * KB + k)
        before = jnp.max(jnp.where(same, e_lane, -1), axis=1, keepdims=True)
        prev = jnp.where(small == k, before, prev)
    prev_v[...] = jnp.where(prev < 0, ZERO, prev)
    last = jnp.broadcast_to(jnp.max(last, axis=0, keepdims=True), (8, 3 * TILE))
    last_v[...] = jnp.where(last < 0, ZERO, last)


def kernel(
    feats_hbm, index_hbm, adj_hbm, weight_hbm, cot_hbm,
    out_hbm, wg_hbm, fg_hbm,
    feats, index, rows8, weight, cot, out, wg_out, fg_out,
    send_v, take_v, slot_v, prev_v, last_v, send_t, take_t, slot_t, prev_t, last_t,
    adj, zb, pk, panel, fwp, fwm, xg, gsend, grecv, gown, grad, pref, pk2, rb, fw2p, fw2m, zs_buf, zrp, zrm,
    wpart, wsib, wy, wz, wx, wt,
    lss, zss, zrs, yss, yrs, xss, xrs, gss, grs, yss2, yrs2, zss2, zrs2, wss, wrs,
):
    r = lax.axis_index("rows")
    x = lax.axis_index("cols")
    z, y, c = r // 8, (r // 2) % 4, r % 2
    me = y * 2 + c

    def dev(dz=0, dy=0, dc=0, dx=0):
        row = ((z + dz) % NZ) * 8 + ((y + dy) % NY) * 2 + (c + dc) % 2
        return {"rows": row, "cols": (x + dx) % NX}

    def rcopy(src, dst, ss, rs, **off):
        return pltpu.make_async_remote_copy(
            src_ref=src, dst_ref=dst, send_sem=ss, recv_sem=rs, device_id=dev(**off), device_id_type=MESH
        )

    def local(n, src, dst):
        cp = pltpu.make_async_copy(src, dst, lss.at[n])
        cp.start()
        return cp

    rows_copy = local(0, index_hbm.at[:, pl.ds(pl.multiple_of(z * 8 * BLK, 8 * BLK), 8 * BLK)], index)
    feats_copy = local(1, feats_hbm, feats)
    peers = [dict(dz=d) for d in range(1, 8)]
    peers += [dict(dy=a, dc=b) for a in range(4) for b in range(2) if (a or b) and (a, b) != (2, 1)]
    peers += [dict(dx=a, dc=b) for a in range(1, 4) for b in range(2)]
    barrier = pltpu.get_barrier_semaphore()
    for off in peers:
        pl.semaphore_signal(barrier, inc=1, device_id=dev(**off), device_id_type=MESH)

    weight_copy = local(2, weight_hbm, weight)
    cot_copy = local(3, cot_hbm, cot)
    adj_copy = local(4, adj_hbm, adj)
    rows_copy.wait()
    rows8[...] = index[...].T
    send_tables(rows8, send_v, take_v, y, z, c, me)
    send_copy = local(5, send_v, send_t)
    take_copy = local(6, take_v, take_t)
    feats_copy.wait()
    for b in range(BLK):
        blk = feats[:, b * TILE:(b + 1) * TILE]
        zb[0][b] = blk
        panel[OWN + b] = blk
    pl.semaphore_wait(barrier, len(peers))

    pending = []
    sent = {}
    done = set()

    half = BLK // 2
    whole = pl.ds(0, BLK)
    zcopies = {}

    def zsend(src, dst, direction, blocks):
        cp = rcopy(zb[src].at[blocks], zb[dst].at[blocks], zss.at[dst + 8 * (direction > 0)], zrs.at[dst + 8 * (direction > 0)], dz=direction)
        cp.start()
        zcopies.setdefault(dst, []).append(cp)
        pending.append(cp)

    def pack(dz, src, put, self_put):
        zs = (z + dz) % NZ

        def one(i, carry):
            dd = ((y + i // 2) % NY) * 2 + (c + i % 2) % 2
            src(i, dd, zs)
            return carry

        lax.fori_loop(0 if self_put else 1, 8, one, 0)

    def ysends(dz, packs, dst_of, fp, fm, ss, rs, copies):
        list_ = []
        for n, (dy, dc) in enumerate(((1, 0), (1, 1), (3, 0), (3, 1), (0, 1))):
            cp = rcopy(packs.at[dz, dy * 2 + dc], dst_of(dz, y), ss.at[dz * 9 + n], rs.at[dz * 9 + n], dy=dy, dc=dc)
            list_.append(cp)
        a = rcopy(packs.at[dz, 4], fp.at[dz], ss.at[dz * 9 + 7], rs.at[dz * 9 + 7], dy=1)
        b = rcopy(packs.at[dz, 5], fm.at[dz], ss.at[dz * 9 + 8], rs.at[dz * 9 + 8], dy=3)
        for cp in (a, b, *list_):
            cp.start()
            pending.append(cp)
        copies[dz] = (list_, a, b)
        sent[dz] = (a, b, *list_)

    def throttle(dz):
        for cp in sent[dz]:
            cp.wait_send()
            done.add(id(cp))

    def forwards(dz, dst_of, fp, fm, ss, rs, copies):
        list_, a, b = copies[dz]
        a.wait_recv()
        f = rcopy(fp.at[dz], dst_of(dz, (y + 3) % NY), ss.at[dz * 9 + 5], rs.at[dz * 9 + 5], dy=1, dc=0)
        f.start()
        b.wait_recv()
        g = rcopy(fm.at[dz], dst_of(dz, (y + 1) % NY), ss.at[dz * 9 + 6], rs.at[dz * 9 + 6], dy=3, dc=1)
        g.start()
        pending.extend((f, g))
        list_ += [f, g]

    def panel_of(dz, yy):
        return panel.at[pl.ds((((z + dz) % NZ) * 8 + yy * 2 + c) * CAP, CAP)]

    ycopies = {}
    zsend(0, 7, 1, whole)
    zsend(0, 1, -1, whole)
    send_copy.wait()
    previous = None
    for at, dz in enumerate(FWD_ORDER):
        if dz:
            for cp in zcopies[dz]:
                cp.wait_recv()
            if dz in (7, 6):
                zsend(dz, dz - 1, 1, whole)
            elif dz == 5:
                zsend(5, 4, 1, pl.ds(0, half))
            elif dz in (1, 2):
                zsend(dz, dz + 1, -1, whole)
            elif dz == 3:
                zsend(3, 4, -1, pl.ds(half, half))

        def message(i, dd, zs, dz=dz):
            for k in range(CAP):
                pk[dz, i, k] = zb[dz][send_t[k * 8 + dd, zs * BLK]]

        pack(dz, message, None, False)
        if dz:
            zs = (z + dz) % NZ
            for k in range(CAP):
                panel[(zs * 8 + me) * CAP + k] = zb[dz][send_t[k * 8 + me, zs * BLK]]
        if FWIN and at >= FWIN:
            throttle(FWD_ORDER[at - FWIN])
        ysends(dz, pk, panel_of, fwp, fwm, yss, yrs, ycopies)
        if at == 0:
            slot_tables(rows8, slot_v, prev_v, last_v, r, me)
            table_copies = [local(7, slot_v, slot_t), local(8, prev_v, prev_t), local(9, last_v, last_t)]
        if previous is not None:
            forwards(previous, panel_of, fwp, fwm, yss, yrs, ycopies)
        previous = dz
    forwards(previous, panel_of, fwp, fwm, yss, yrs, ycopies)
    weight_copy.wait()
    w_all = jnp.concatenate(
        [weight[pl.ds(pl.multiple_of(((x + dx) % NX) * FR, FR), FR)] for dx in range(NX)], axis=0
    )
    unit = lax.broadcasted_iota(jnp.int32, (UR, NX * UR), 1) - lax.broadcasted_iota(jnp.int32, (UR, NX * UR), 0)
    pick = jnp.where(unit == x * UR, 1.0, 0.0).astype(BF16)
    w_rows = lax.dot_general(w_all, pick, NT, preferred_element_type=F32).astype(BF16)
    w_cols = lax.dot_general(pick, w_all, NT, preferred_element_type=F32).astype(BF16)
    for cp in (take_copy, *table_copies, cot_copy, adj_copy):
        cp.wait()
    for dz in FWD_ORDER:
        for cp in ycopies[dz][0]:
            cp.wait_recv()

    xcopies = {}
    for q in range(CH):

        def block(n, carry, q=q):
            i = q * (BLK // CH) + n
            acc = jnp.zeros((TILE, FR), F32)
            for k in range(0, KB, 2):
                left = jnp.concatenate([adj[i * KB + k], adj[i * KB + k + 1]], axis=1)
                right = jnp.concatenate([panel[slot_t[i, k]], panel[slot_t[i, k + 1]]], axis=1)
                acc += lax.dot_general(left, right, NT, preferred_element_type=F32)
            xg[0, q, :, pl.ds(pl.multiple_of(n * TILE, TILE), TILE)] = acc.T.astype(BF16)
            return carry

        lax.fori_loop(0, BLK // CH, block, 0)
        for dx in (2, 1, 3):
            cp = rcopy(xg.at[0, q], xg.at[4 - dx, q], xss.at[q * 4 + dx], xrs.at[q * 4 + dx], dx=dx)
            cp.start()
            pending.append(cp)
            xcopies[q, dx] = cp

    gcopies = {}
    out_copies = []
    for q in range(CH):
        cols = pl.ds(q * CN, CN)
        for dx in (1, 3, 2):
            xcopies[q, dx].wait_recv()
        agg = xg[:, q].reshape(NX * FR, CN)
        pre = jnp.dot(w_cols, agg, preferred_element_type=F32)
        sig = jax.nn.sigmoid(pre)
        out[:, cols] = (pre * sig).astype(BF16)
        out_copies.append(local(10 + q, out.at[:, cols], out_hbm.at[:, cols]))
        pg = (cot[:, cols].astype(F32) * sig * (1.0 + pre * (1.0 - sig))).astype(BF16)
        part = jnp.dot(w_rows, pg, preferred_element_type=F32)
        gown[q] = part[0:FR]
        for dx in (2, 1, 3):
            gsend[dx, q] = part[dx * FR:(dx + 1) * FR].astype(BF16)
            cp = rcopy(gsend.at[dx, q], grecv.at[4 - dx, q], gss.at[q * 4 + dx], grs.at[q * 4 + dx], dx=dx)
            cp.start()
            pending.append(cp)
            gcopies[q, dx] = cp
        wg = lax.dot_general(pg, agg, NT, preferred_element_type=F32)
        if q == 0:
            wpart[...] = wg
        else:
            wpart[...] += wg

    hu = UR // 2
    w1 = rcopy(wpart.at[pl.ds(pl.multiple_of((1 - c) * hu, 8), hu)], wsib, wss.at[0], wrs.at[0], dc=1)
    w1.start()
    pending.append(w1)

    for q in range(CH):
        for dx in (1, 3, 2):
            gcopies[q, dx].wait_recv()
        g = gown[q] + grecv[1, q].astype(F32) + grecv[2, q].astype(F32) + grecv[3, q].astype(F32)
        g = g.astype(BF16)
        for n in range(BLK // CH):
            grad[q * (BLK // CH) + n] = g[:, n * TILE:(n + 1) * TILE]

    w1.wait_recv()
    wy[y] = wpart[pl.ds(pl.multiple_of(c * hu, 8), hu)] + wsib[...]
    w2 = []
    for dy in (1, 2, 3):
        cp = rcopy(wy.at[y], wy.at[y], wss.at[dy], wrs.at[dy], dy=dy)
        cp.start()
        pending.append(cp)
        w2.append(cp)

    pref[ZERO] = jnp.zeros((FR, TILE), F32)

    def terms(i, carry):
        g = grad[i]
        for k in range(0, KB, 2):
            e = i * KB + k
            pair = jnp.concatenate([adj[e], adj[e + 1]], axis=1)
            term = jnp.dot(g, pair, preferred_element_type=F32)
            pref[e] = term[:, :TILE] + pref[prev_t[i, k]]
            pref[e + 1] = term[:, TILE:] + pref[prev_t[i, k + 1]]
        return carry

    lax.fori_loop(0, BLK, terms, 0)

    for cp in w2:
        cp.wait_recv()
    wz[z] = (wy[0] + wy[1]) + (wy[2] + wy[3])
    w3 = []
    for dz in range(1, NZ):
        cp = rcopy(wz.at[z], wz.at[z], wss.at[3 + dz], wrs.at[3 + dz], dz=dz)
        cp.start()
        pending.append(cp)
        w3.append(cp)

    ycopies2 = {}

    def rb_of(dz, yy):
        return rb[dz].at[pl.ds((yy * 2 + c) * CAP, CAP)]

    for dz in range(NZ):
        rb[dz][8 * CAP] = jnp.zeros((FR, TILE), BF16)
    zin = {}

    def reduce_chunk(dz):
        for cp in ycopies2[dz][0]:
            cp.wait_recv()
        for cp in zin.get(dz, ()):
            cp.wait_recv()
        zs = (z + dz) % NZ

        def total(b, carry, dz=dz, zs=zs):
            acc = jnp.zeros((FR, TILE), F32)
            for n in range(8):
                acc += rb[dz][take_t[n, zs * BLK + b]].astype(F32)
            if dz in (1, 2):
                acc += zrp[dz, b].astype(F32)
            if dz in (6, 7):
                acc += zrm[dz, b].astype(F32)
            if dz == 0:
                acc += zrp[0, b].astype(F32) + zrm[0, b].astype(F32) + pref[last_t[0, OWN + b]]
                fg_out[:, pl.ds(pl.multiple_of(b * TILE, TILE), TILE)] = acc
            else:
                zs_buf[dz, b] = acc.astype(BF16)
            return carry

        def total_more(b, carry, dz=dz, zs=zs):
            off = 0 if dz == 3 else half
            acc = (zrp if dz == 3 else zrm)[dz, off + b].astype(F32)
            for n in range(8):
                acc += rb[dz][take_t[n, zs * BLK + off + b]].astype(F32)
            zs_buf[dz, off + b] = acc.astype(BF16)
            return carry

        def total_less(b, carry, dz=dz, zs=zs):
            off = half if dz == 3 else 0
            acc = jnp.zeros((FR, TILE), F32)
            for n in range(8):
                acc += rb[dz][take_t[n, zs * BLK + off + b]].astype(F32)
            zs_buf[dz, off + b] = acc.astype(BF16)
            return carry

        if dz in (3, 5):
            lax.fori_loop(0, half, total_more, 0)
            lax.fori_loop(0, half, total_less, 0)
        else:
            lax.fori_loop(0, BLK, total, 0)

        def ring(direction, blocks):
            to = dz - direction if dz - direction != 8 else 0
            buf = zrp if direction > 0 else zrm
            n = dz + 8 * (direction > 0)
            cp = rcopy(zs_buf.at[dz, blocks], buf.at[to, blocks], zss2.at[n], zrs2.at[n], dz=direction)
            cp.start()
            pending.append(cp)
            zin.setdefault(to, []).append(cp)

        if dz == 4:
            ring(1, pl.ds(0, half))
            ring(-1, pl.ds(half, half))
        elif dz in (1, 2, 3):
            ring(1, whole)
        elif dz in (5, 6, 7):
            ring(-1, whole)

    def weight_cols():
        for cp in w3:
            cp.wait_recv()
        wx[0, c] = (((wz[0] + wz[1]) + (wz[2] + wz[3])) + ((wz[4] + wz[5]) + (wz[6] + wz[7]))) * (
            1.0 / math.sqrt(NODES_DEV * 64)
        )
        w4 = []
        for dx in range(4):
            for dc in range(2):
                if dx or dc:
                    n = 11 + dx * 2 + dc
                    cp = rcopy(wx.at[0, c], wx.at[(4 - dx) % 4, c], wss.at[n], wrs.at[n], dx=dx, dc=dc)
                    cp.start()
                    pending.append(cp)
                    w4.append(cp)
        return w4

    sent.clear()
    for at, dz in enumerate(BWD_ORDER):

        def term(i, dd, zs, dz=dz):
            for k in range(CAP):
                pk2[dz, i, k] = pref[last_t[0, (zs * 8 + dd) * CAP + k]].astype(BF16)

        pack(dz, term, None, False)
        zs = (z + dz) % NZ
        for k in range(CAP):
            if dz:
                rb[dz][me * CAP + k] = pref[last_t[0, (zs * 8 + me) * CAP + k]].astype(BF16)
            else:
                rb[dz][me * CAP + k] = jnp.zeros((FR, TILE), BF16)
        if BWIN and at >= BWIN:
            throttle(BWD_ORDER[at - BWIN])
        ysends(dz, pk2, rb_of, fw2p, fw2m, yss2, yrs2, ycopies2)
        if at:
            forwards(BWD_ORDER[at - 1], rb_of, fw2p, fw2m, yss2, yrs2, ycopies2)
        if at == 3:
            w4 = weight_cols()
        if at >= LAG:
            reduce_chunk(BWD_ORDER[at - LAG])
    forwards(0, rb_of, fw2p, fw2m, yss2, yrs2, ycopies2)
    for dz in BWD_ORDER[NZ - LAG:]:
        reduce_chunk(dz)

    for cp in w4:
        cp.wait_recv()
    for dx in range(4):
        for cc in range(2):
            f0 = ((4 - dx) % 4) * FR
            row = pl.multiple_of(((x + dx) % NX) * UR + cc * hu, 8)
            wt[pl.ds(row, hu), 0:FR] = wx[dx, cc][:, f0:f0 + FR]
    wg_out[...] = wt[...].T[0:FR]
    out_copies += [local(14, wg_out, wg_hbm), local(15, fg_out, fg_hbm)]
    for cp in out_copies:
        cp.wait()

    for cp in pending:
        if id(cp) not in done:
            cp.wait_send()


def keep(a, b, c, a_out, b_out, c_out):
    a_out[...] = a[...]
    b_out[...] = b[...]
    c_out[...] = c[...]


def body(feats_t, adj_index, adj_weight, weight, cotangent_t):
    hbm = pl.BlockSpec(memory_space=pl.ANY)
    dma = pltpu.SemaphoreType.DMA
    blk = (FR, TILE)
    V = pltpu.VMEM
    table = lambda space: [space(s, jnp.int32) for s in ((4 * 8, TILE), (8, TILE), (BLK, TILE), (BLK, TILE), (8, 3 * TILE))]
    shapes = (
        jax.ShapeDtypeStruct((UR, NODES_DEV), BF16),
        jax.ShapeDtypeStruct((FR, NX * UR), F32),
        jax.ShapeDtypeStruct((FR, NODES_DEV), F32),
    )
    outs = pl.pallas_call(
        kernel,
        out_shape=shapes,
        in_specs=[hbm] * 5,
        out_specs=(hbm,) * 3,
        scratch_shapes=[
            V((FR, NODES_DEV), BF16),
            V((KB, 8 * BLK), jnp.int32),
            V((8 * BLK, KB), jnp.int32),
            V((NX * FR, NX * UR), BF16),
            V((UR, NODES_DEV), BF16),
            V((UR, NODES_DEV), BF16),
            V((FR, NX * UR), F32),
            V((FR, NODES_DEV), F32),
            *table(V),
            *table(pltpu.SMEM),
            V((BLK * KB, TILE, TILE), BF16),
            [V((BLK, *blk), BF16) for _ in range(NZ)],
            V((NZ, 8, CAP, *blk), BF16),
            V((OWN + BLK, *blk), BF16),
            V((NZ, CAP, *blk), BF16),
            V((NZ, CAP, *blk), BF16),
            V((NX, CH, FR, CN), BF16),
            V((NX, CH, FR, CN), BF16),
            V((NX, CH, FR, CN), BF16),
            V((CH, FR, CN), F32),
            V((BLK, *blk), BF16),
            V((BLK * KB + 1, *blk), F32),
            V((NZ, 8, CAP, *blk), BF16),
            [V((8 * CAP + 1, *blk), BF16) for _ in range(NZ)],
            V((NZ, CAP, *blk), BF16),
            V((NZ, CAP, *blk), BF16),
            V((NZ, BLK, *blk), BF16),
            V((NZ, BLK, *blk), BF16),
            V((NZ, BLK, *blk), BF16),
            V((UR, NX * FR), F32),
            V((UR // 2, NX * FR), F32),
            V((NY, UR // 2, NX * FR), F32),
            V((NZ, UR // 2, NX * FR), F32),
            V((NX, NC, UR // 2, NX * FR), F32),
            V((NX * UR, TILE), F32),
            dma((16,)),
            dma((16,)),
            dma((16,)),
            dma((9 * NZ,)),
            dma((9 * NZ,)),
            dma((16,)),
            dma((16,)),
            dma((16,)),
            dma((16,)),
            dma((9 * NZ,)),
            dma((9 * NZ,)),
            dma((16,)),
            dma((16,)),
            dma((19,)),
            dma((19,)),
        ],
        compiler_params=pltpu.CompilerParams(
            collective_id=0, has_side_effects=True, vmem_limit_bytes=56 * 2**20
        ),
        name="gcn_step",
    )(feats_t, adj_index.T, adj_weight.reshape(BLK * KB, TILE, TILE), weight, cotangent_t)
    return pl.pallas_call(
        keep,
        out_shape=shapes,
        name="results",
    )(*outs)


def solution(mesh):
    return jax.shard_map(
        body,
        mesh=mesh,
        in_specs=(P("cols", "rows"), P(), P("rows", None, None, None), P(), P("cols", "rows")),
        out_specs=(P("cols", "rows"), P("cols", None), P("cols", "rows")),
        check_vma=False,
    )
```

```python
import math

import jax
import jax.numpy as jnp
from jax import lax
from jax.experimental import pallas as pl
from jax.experimental.pallas import tpu as pltpu
from jax.sharding import PartitionSpec as P

MESH = pl.DeviceIdType.MESH
NZ, NY, NC, NX = 8, 4, 2, 4
BLK, KB, TILE, CAP, FR, UR = 16, 16, 128, 4, 32, 64
NODES_DEV = BLK * TILE
CH = 4
CN = NODES_DEV // CH
OWN = 64 * CAP
ZERO = BLK * KB
FWD_ORDER = (0, 7, 1, 6, 2, 5, 3, 4)
BWD_ORDER = (4, 3, 5, 2, 6, 1, 7, 0)
FWIN, BWIN, LAG = 2, 2, 3
F32, BF16 = jnp.float32, jnp.bfloat16
NT = (((1,), (1,)), ((), ()))


def group_sum(v, lane):
    n = v.shape[1]
    for step in (1, 2, 4, 8):
        up = pltpu.roll(v, n - step, 1)
        down = pltpu.roll(v, step, 1)
        v = v + jnp.where((lane & step) == 0, up, down)
    return v


def group_rank(named, lane):
    rank = jnp.zeros_like(named)
    for step in range(1, BLK):
        rank = rank + jnp.where((lane & (BLK - 1)) >= step, pltpu.roll(named, step, 1), 0)
    return rank


def send_tables(rows8, send_v, take_v, y, z, c, me):
    lane = lax.broadcasted_iota(jnp.int32, (8 * BLK, TILE), 1)
    target = (lane >> 4) * (8 * BLK) + (lane & 15) + (y * 2 + c) * BLK
    hit = jnp.zeros((8 * BLK, TILE), jnp.int32)
    for k in range(KB):
        hit = jnp.where(rows8[:, k:k + 1] == target, 1, hit)
    named = jnp.max(hit.reshape(8, BLK, TILE), axis=1)
    lane = lax.broadcasted_iota(jnp.int32, (8, TILE), 1)
    rank = group_rank(named, lane)
    for k in range(CAP):
        send_v[k * 8:(k + 1) * 8] = group_sum(jnp.where((named > 0) & (rank == k), lane & 15, 0), lane)
    d = lax.broadcasted_iota(jnp.int32, (8, TILE), 0)
    use = (named > 0) & ((d != me) | ((lane >> 4) != z))
    take_v[...] = jnp.where(use, d * CAP + jnp.minimum(rank, CAP - 1), 8 * CAP)


def slot_tables(rows8, slot_v, prev_v, last_v, r, me):
    own = rows8[pl.ds(pl.multiple_of(me * BLK, BLK), BLK)]
    lane = lax.broadcasted_iota(jnp.int32, (BLK, 64 * BLK), 1)
    hit = jnp.zeros((BLK, 64 * BLK), jnp.int32)
    for k in range(KB):
        hit = jnp.where(own[:, k:k + 1] == lane, 1, hit)
    lane8 = lax.broadcasted_iota(jnp.int32, (8, 64 * BLK), 1)
    named = jnp.broadcast_to(jnp.max(hit, axis=0, keepdims=True), (8, 64 * BLK))
    value = (lane8 >> 4) * CAP + jnp.minimum(group_rank(named, lane8), CAP - 1)
    value = jnp.where((lane8 >> 4) == r, OWN + (lane8 & 15), value)
    value = jnp.concatenate([value, value], axis=0)
    small = lax.broadcasted_iota(jnp.int32, (BLK, TILE), 1)
    e_lane = lax.broadcasted_iota(jnp.int32, (BLK, BLK * KB), 1)
    row = lax.broadcasted_iota(jnp.int32, (BLK, BLK * KB), 0)
    t_lane = lax.broadcasted_iota(jnp.int32, (BLK, 3 * TILE), 1)
    t_row = lax.broadcasted_iota(jnp.int32, (BLK, 3 * TILE), 0)
    slots = jnp.zeros((BLK, TILE), jnp.int32)
    spread = jnp.zeros((BLK, BLK * KB), jnp.int32)
    last = jnp.full((BLK, 3 * TILE), -1, jnp.int32)
    columns = []
    for k in range(KB):
        col = jnp.max(jnp.where(own[:, k:k + 1] == lane, value, 0), axis=1, keepdims=True)
        columns.append(col)
        slots = jnp.where(small == k, col, slots)
        spread = jnp.where((e_lane & 15) == k, col, spread)
        last = jnp.maximum(last, jnp.where(col == t_lane, t_row * KB + k, -1))
    slot_v[...] = slots
    by_lane = jnp.max(jnp.where((e_lane >> 4) == row, spread, 0), axis=0, keepdims=True)
    prev = jnp.zeros((BLK, TILE), jnp.int32)
    for k in range(KB):
        same = (columns[k] == by_lane) & (e_lane < row * KB + k)
        before = jnp.max(jnp.where(same, e_lane, -1), axis=1, keepdims=True)
        prev = jnp.where(small == k, before, prev)
    prev_v[...] = jnp.where(prev < 0, ZERO, prev)
    last = jnp.broadcast_to(jnp.max(last, axis=0, keepdims=True), (8, 3 * TILE))
    last_v[...] = jnp.where(last < 0, ZERO, last)


def kernel(
    feats_hbm, index_hbm, adj_hbm, weight_hbm, cot_hbm,
    out_hbm, wg_hbm, fg_hbm,
    feats, index, rows8, weight, cot, out, wg_out, fg_out,
    send_v, take_v, slot_v, prev_v, last_v, send_t, take_t, slot_t, prev_t, last_t,
    adj, zb, pk, panel, fwp, fwm, xg, gsend, grecv, gown, grad, pref, pk2, rb, fw2p, fw2m, zs_buf, zrp, zrm,
    wpart, wsib, wy, wz, wx, wt,
    lss, zss, zrs, yss, yrs, xss, xrs, gss, grs, yss2, yrs2, zss2, zrs2, wss, wrs,
):
    r = lax.axis_index("rows")
    x = lax.axis_index("cols")
    z, y, c = r // 8, (r // 2) % 4, r % 2
    me = y * 2 + c

    def dev(dz=0, dy=0, dc=0, dx=0):
        row = ((z + dz) % NZ) * 8 + ((y + dy) % NY) * 2 + (c + dc) % 2
        return {"rows": row, "cols": (x + dx) % NX}

    def rcopy(src, dst, ss, rs, **off):
        return pltpu.make_async_remote_copy(
            src_ref=src, dst_ref=dst, send_sem=ss, recv_sem=rs, device_id=dev(**off), device_id_type=MESH
        )

    def local(n, src, dst):
        cp = pltpu.make_async_copy(src, dst, lss.at[n])
        cp.start()
        return cp

    rows_copy = local(0, index_hbm.at[:, pl.ds(pl.multiple_of(z * 8 * BLK, 8 * BLK), 8 * BLK)], index)
    feats_copy = local(1, feats_hbm, feats)
    peers = [dict(dz=d) for d in range(1, 8)]
    peers += [dict(dy=a, dc=b) for a in range(4) for b in range(2) if (a or b) and (a, b) != (2, 1)]
    peers += [dict(dx=a, dc=b) for a in range(1, 4) for b in range(2)]
    barrier = pltpu.get_barrier_semaphore()
    for off in peers:
        pl.semaphore_signal(barrier, inc=1, device_id=dev(**off), device_id_type=MESH)

    weight_copy = local(2, weight_hbm, weight)
    cot_copy = local(3, cot_hbm, cot)
    adj_copy = local(4, adj_hbm, adj)
    rows_copy.wait()
    rows8[...] = index[...].T
    send_tables(rows8, send_v, take_v, y, z, c, me)
    send_copy = local(5, send_v, send_t)
    take_copy = local(6, take_v, take_t)
    feats_copy.wait()
    for b in range(BLK):
        blk = feats[:, b * TILE:(b + 1) * TILE]
        zb[0][b] = blk
        panel[OWN + b] = blk
    pl.semaphore_wait(barrier, len(peers))

    pending = []
    sent = {}
    done = set()

    half = BLK // 2
    whole = pl.ds(0, BLK)
    zcopies = {}

    def zsend(src, dst, direction, blocks):
        cp = rcopy(zb[src].at[blocks], zb[dst].at[blocks], zss.at[dst + 8 * (direction > 0)], zrs.at[dst + 8 * (direction > 0)], dz=direction)
        cp.start()
        zcopies.setdefault(dst, []).append(cp)
        pending.append(cp)

    def pack(dz, src, put, self_put):
        zs = (z + dz) % NZ

        def one(i, carry):
            dd = ((y + i // 2) % NY) * 2 + (c + i % 2) % 2
            src(i, dd, zs)
            return carry

        lax.fori_loop(0 if self_put else 1, 8, one, 0)

    def ysends(dz, packs, dst_of, fp, fm, ss, rs, copies):
        list_ = []
        for n, (dy, dc) in enumerate(((1, 0), (1, 1), (3, 0), (3, 1), (0, 1))):
            cp = rcopy(packs.at[dz, dy * 2 + dc], dst_of(dz, y), ss.at[dz * 9 + n], rs.at[dz * 9 + n], dy=dy, dc=dc)
            list_.append(cp)
        a = rcopy(packs.at[dz, 4], fp.at[dz], ss.at[dz * 9 + 7], rs.at[dz * 9 + 7], dy=1)
        b = rcopy(packs.at[dz, 5], fm.at[dz], ss.at[dz * 9 + 8], rs.at[dz * 9 + 8], dy=3)
        for cp in (a, b, *list_):
            cp.start()
            pending.append(cp)
        copies[dz] = (list_, a, b)
        sent[dz] = (a, b, *list_)

    def throttle(dz):
        for cp in sent[dz]:
            cp.wait_send()
            done.add(id(cp))

    def forwards(dz, dst_of, fp, fm, ss, rs, copies):
        list_, a, b = copies[dz]
        a.wait_recv()
        f = rcopy(fp.at[dz], dst_of(dz, (y + 3) % NY), ss.at[dz * 9 + 5], rs.at[dz * 9 + 5], dy=1, dc=0)
        f.start()
        b.wait_recv()
        g = rcopy(fm.at[dz], dst_of(dz, (y + 1) % NY), ss.at[dz * 9 + 6], rs.at[dz * 9 + 6], dy=3, dc=1)
        g.start()
        pending.extend((f, g))
        list_ += [f, g]

    def panel_of(dz, yy):
        return panel.at[pl.ds((((z + dz) % NZ) * 8 + yy * 2 + c) * CAP, CAP)]

    ycopies = {}
    zsend(0, 7, 1, whole)
    zsend(0, 1, -1, whole)
    send_copy.wait()
    previous = None
    for at, dz in enumerate(FWD_ORDER):
        if dz:
            for cp in zcopies[dz]:
                cp.wait_recv()
            if dz in (7, 6):
                zsend(dz, dz - 1, 1, whole)
            elif dz == 5:
                zsend(5, 4, 1, pl.ds(0, half))
            elif dz in (1, 2):
                zsend(dz, dz + 1, -1, whole)
            elif dz == 3:
                zsend(3, 4, -1, pl.ds(half, half))

        def message(i, dd, zs, dz=dz):
            for k in range(CAP):
                pk[dz, i, k] = zb[dz][send_t[k * 8 + dd, zs * BLK]]

        pack(dz, message, None, False)
        if dz:
            zs = (z + dz) % NZ
            for k in range(CAP):
                panel[(zs * 8 + me) * CAP + k] = zb[dz][send_t[k * 8 + me, zs * BLK]]
        if FWIN and at >= FWIN:
            throttle(FWD_ORDER[at - FWIN])
        ysends(dz, pk, panel_of, fwp, fwm, yss, yrs, ycopies)
        if at == 0:
            slot_tables(rows8, slot_v, prev_v, last_v, r, me)
            table_copies = [local(7, slot_v, slot_t), local(8, prev_v, prev_t), local(9, last_v, last_t)]
        if previous is not None:
            forwards(previous, panel_of, fwp, fwm, yss, yrs, ycopies)
        previous = dz
    forwards(previous, panel_of, fwp, fwm, yss, yrs, ycopies)
    weight_copy.wait()
    w_all = jnp.concatenate(
        [weight[pl.ds(pl.multiple_of(((x + dx) % NX) * FR, FR), FR)] for dx in range(NX)], axis=0
    )
    unit = lax.broadcasted_iota(jnp.int32, (UR, NX * UR), 1) - lax.broadcasted_iota(jnp.int32, (UR, NX * UR), 0)
    pick = jnp.where(unit == x * UR, 1.0, 0.0).astype(BF16)
    w_rows = lax.dot_general(w_all, pick, NT, preferred_element_type=F32).astype(BF16)
    w_cols = lax.dot_general(pick, w_all, NT, preferred_element_type=F32).astype(BF16)
    for cp in (take_copy, *table_copies, cot_copy, adj_copy):
        cp.wait()
    for dz in FWD_ORDER:
        for cp in ycopies[dz][0]:
            cp.wait_recv()

    xcopies = {}
    for q in range(CH):

        def block(n, carry, q=q):
            i = q * (BLK // CH) + n
            acc = jnp.zeros((TILE, FR), F32)
            for k in range(0, KB, 2):
                left = jnp.concatenate([adj[i * KB + k], adj[i * KB + k + 1]], axis=1)
                right = jnp.concatenate([panel[slot_t[i, k]], panel[slot_t[i, k + 1]]], axis=1)
                acc += lax.dot_general(left, right, NT, preferred_element_type=F32)
            xg[0, q, :, pl.ds(pl.multiple_of(n * TILE, TILE), TILE)] = acc.T.astype(BF16)
            return carry

        lax.fori_loop(0, BLK // CH, block, 0)
        for dx in (2, 1, 3):
            cp = rcopy(xg.at[0, q], xg.at[4 - dx, q], xss.at[q * 4 + dx], xrs.at[q * 4 + dx], dx=dx)
            cp.start()
            pending.append(cp)
            xcopies[q, dx] = cp

    gcopies = {}
    out_copies = []
    for q in range(CH):
        cols = pl.ds(q * CN, CN)
        for dx in (1, 3, 2):
            xcopies[q, dx].wait_recv()
        agg = xg[:, q].reshape(NX * FR, CN)
        pre = jnp.dot(w_cols, agg, preferred_element_type=F32)
        sig = jax.nn.sigmoid(pre)
        out[:, cols] = (pre * sig).astype(BF16)
        out_copies.append(local(10 + q, out.at[:, cols], out_hbm.at[:, cols]))
        pg = (cot[:, cols].astype(F32) * sig * (1.0 + pre * (1.0 - sig))).astype(BF16)
        part = jnp.dot(w_rows, pg, preferred_element_type=F32)
        gown[q] = part[0:FR]
        for dx in (2, 1, 3):
            gsend[dx, q] = part[dx * FR:(dx + 1) * FR].astype(BF16)
            cp = rcopy(gsend.at[dx, q], grecv.at[4 - dx, q], gss.at[q * 4 + dx], grs.at[q * 4 + dx], dx=dx)
            cp.start()
            pending.append(cp)
            gcopies[q, dx] = cp
        wg = lax.dot_general(pg, agg, NT, preferred_element_type=F32)
        if q == 0:
            wpart[...] = wg
        else:
            wpart[...] += wg

    hu = UR // 2
    w1 = rcopy(wpart.at[pl.ds(pl.multiple_of((1 - c) * hu, 8), hu)], wsib, wss.at[0], wrs.at[0], dc=1)
    w1.start()
    pending.append(w1)

    pref[ZERO] = jnp.zeros((FR, TILE), F32)

    def terms(i, carry):
        g = grad[i]
        for k in range(0, KB, 2):
            e = i * KB + k
            pair = jnp.concatenate([adj[e], adj[e + 1]], axis=1)
            term = jnp.dot(g, pair, preferred_element_type=F32)
            pref[e] = term[:, :TILE] + pref[prev_t[i, k]]
            pref[e + 1] = term[:, TILE:] + pref[prev_t[i, k + 1]]
        return carry

    nb = BLK // CH
    for q in range(CH):
        for dx in (1, 3, 2):
            gcopies[q, dx].wait_recv()
        g = gown[q] + grecv[1, q].astype(F32) + grecv[2, q].astype(F32) + grecv[3, q].astype(F32)
        g = g.astype(BF16)
        for n in range(nb):
            grad[q * nb + n] = g[:, n * TILE:(n + 1) * TILE]
        lax.fori_loop(q * nb, (q + 1) * nb, terms, 0)
        if q == 1:
            w1.wait_recv()
            wy[y] = wpart[pl.ds(pl.multiple_of(c * hu, 8), hu)] + wsib[...]
            w2 = []
            for dy in (1, 2, 3):
                cp = rcopy(wy.at[y], wy.at[y], wss.at[dy], wrs.at[dy], dy=dy)
                cp.start()
                pending.append(cp)
                w2.append(cp)


    for cp in w2:
        cp.wait_recv()
    wz[z] = (wy[0] + wy[1]) + (wy[2] + wy[3])
    w3 = []
    for dz in range(1, NZ):
        cp = rcopy(wz.at[z], wz.at[z], wss.at[3 + dz], wrs.at[3 + dz], dz=dz)
        cp.start()
        pending.append(cp)
        w3.append(cp)

    ycopies2 = {}

    def rb_of(dz, yy):
        return rb[dz].at[pl.ds((yy * 2 + c) * CAP, CAP)]

    for dz in range(NZ):
        rb[dz][8 * CAP] = jnp.zeros((FR, TILE), BF16)
    zin = {}

    def reduce_chunk(dz):
        for cp in ycopies2[dz][0]:
            cp.wait_recv()
        zs = (z + dz) % NZ
        for h in ((1, 0) if dz == 3 else (0, 1)):
            arrived = []
            for cp, buf in zin.get((dz, h), ()):
                cp.wait_recv()
                arrived.append(buf)

            def total(n, carry, h=h, arrived=tuple(arrived)):
                b = h * half + n
                acc = jnp.zeros((FR, TILE), F32)
                for d in range(8):
                    acc += rb[dz][take_t[d, zs * BLK + b]].astype(F32)
                for buf in arrived:
                    acc += buf[dz, b].astype(F32)
                if dz:
                    zs_buf[dz, b] = acc.astype(BF16)
                else:
                    acc += pref[last_t[0, OWN + b]]
                    fg_out[:, pl.ds(pl.multiple_of(b * TILE, TILE), TILE)] = acc
                return carry

            lax.fori_loop(0, half, total, 0)
            if dz:
                up = dz < 4 or (dz == 4 and h == 0)
                to = dz - 1 if up else (dz + 1) % NZ
                buf = zrp if up else zrm
                blocks = pl.ds(h * half, half)
                n = dz * 2 + h
                cp = rcopy(zs_buf.at[dz, blocks], buf.at[to, blocks], zss2.at[n], zrs2.at[n], dz=1 if up else -1)
                cp.start()
                pending.append(cp)
                zin.setdefault((to, h), []).append((cp, buf))

    def weight_cols():
        for cp in w3:
            cp.wait_recv()
        wx[0, c] = (((wz[0] + wz[1]) + (wz[2] + wz[3])) + ((wz[4] + wz[5]) + (wz[6] + wz[7]))) * (
            1.0 / math.sqrt(NODES_DEV * 64)
        )
        w4 = []
        for dx in range(4):
            for dc in range(2):
                if dx or dc:
                    n = 11 + dx * 2 + dc
                    cp = rcopy(wx.at[0, c], wx.at[(4 - dx) % 4, c], wss.at[n], wrs.at[n], dx=dx, dc=dc)
                    cp.start()
                    pending.append(cp)
                    w4.append(cp)
        return w4

    sent.clear()
    for at, dz in enumerate(BWD_ORDER):

        def term(i, dd, zs, dz=dz):
            for k in range(CAP):
                pk2[dz, i, k] = pref[last_t[0, (zs * 8 + dd) * CAP + k]].astype(BF16)

        pack(dz, term, None, False)
        zs = (z + dz) % NZ
        for k in range(CAP):
            if dz:
                rb[dz][me * CAP + k] = pref[last_t[0, (zs * 8 + me) * CAP + k]].astype(BF16)
            else:
                rb[dz][me * CAP + k] = jnp.zeros((FR, TILE), BF16)
        if BWIN and at >= BWIN:
            throttle(BWD_ORDER[at - BWIN])
        ysends(dz, pk2, rb_of, fw2p, fw2m, yss2, yrs2, ycopies2)
        if at:
            forwards(BWD_ORDER[at - 1], rb_of, fw2p, fw2m, yss2, yrs2, ycopies2)
        if at == 3:
            w4 = weight_cols()
        if at >= LAG:
            reduce_chunk(BWD_ORDER[at - LAG])
    forwards(0, rb_of, fw2p, fw2m, yss2, yrs2, ycopies2)
    for dz in BWD_ORDER[NZ - LAG:]:
        reduce_chunk(dz)

    for cp in w4:
        cp.wait_recv()
    for dx in range(4):
        for cc in range(2):
            f0 = ((4 - dx) % 4) * FR
            row = pl.multiple_of(((x + dx) % NX) * UR + cc * hu, 8)
            wt[pl.ds(row, hu), 0:FR] = wx[dx, cc][:, f0:f0 + FR]
    wg_out[...] = wt[...].T[0:FR]
    out_copies += [local(14, wg_out, wg_hbm), local(15, fg_out, fg_hbm)]
    for cp in out_copies:
        cp.wait()

    for cp in pending:
        if id(cp) not in done:
            cp.wait_send()


def keep(a, b, c, a_out, b_out, c_out):
    a_out[...] = a[...]
    b_out[...] = b[...]
    c_out[...] = c[...]


def body(feats_t, adj_index, adj_weight, weight, cotangent_t):
    hbm = pl.BlockSpec(memory_space=pl.ANY)
    dma = pltpu.SemaphoreType.DMA
    blk = (FR, TILE)
    V = pltpu.VMEM
    table = lambda space: [space(s, jnp.int32) for s in ((4 * 8, TILE), (8, TILE), (BLK, TILE), (BLK, TILE), (8, 3 * TILE))]
    shapes = (
        jax.ShapeDtypeStruct((UR, NODES_DEV), BF16),
        jax.ShapeDtypeStruct((FR, NX * UR), F32),
        jax.ShapeDtypeStruct((FR, NODES_DEV), F32),
    )
    outs = pl.pallas_call(
        kernel,
        out_shape=shapes,
        in_specs=[hbm] * 5,
        out_specs=(hbm,) * 3,
        scratch_shapes=[
            V((FR, NODES_DEV), BF16),
            V((KB, 8 * BLK), jnp.int32),
            V((8 * BLK, KB), jnp.int32),
            V((NX * FR, NX * UR), BF16),
            V((UR, NODES_DEV), BF16),
            V((UR, NODES_DEV), BF16),
            V((FR, NX * UR), F32),
            V((FR, NODES_DEV), F32),
            *table(V),
            *table(pltpu.SMEM),
            V((BLK * KB, TILE, TILE), BF16),
            [V((BLK, *blk), BF16) for _ in range(NZ)],
            V((NZ, 8, CAP, *blk), BF16),
            V((OWN + BLK, *blk), BF16),
            V((NZ, CAP, *blk), BF16),
            V((NZ, CAP, *blk), BF16),
            V((NX, CH, FR, CN), BF16),
            V((NX, CH, FR, CN), BF16),
            V((NX, CH, FR, CN), BF16),
            V((CH, FR, CN), F32),
            V((BLK, *blk), BF16),
            V((BLK * KB + 1, *blk), F32),
            V((NZ, 8, CAP, *blk), BF16),
            [V((8 * CAP + 1, *blk), BF16) for _ in range(NZ)],
            V((NZ, CAP, *blk), BF16),
            V((NZ, CAP, *blk), BF16),
            V((NZ, BLK, *blk), BF16),
            V((NZ, BLK, *blk), BF16),
            V((NZ, BLK, *blk), BF16),
            V((UR, NX * FR), F32),
            V((UR // 2, NX * FR), F32),
            V((NY, UR // 2, NX * FR), F32),
            V((NZ, UR // 2, NX * FR), F32),
            V((NX, NC, UR // 2, NX * FR), F32),
            V((NX * UR, TILE), F32),
            dma((16,)),
            dma((16,)),
            dma((16,)),
            dma((9 * NZ,)),
            dma((9 * NZ,)),
            dma((16,)),
            dma((16,)),
            dma((16,)),
            dma((16,)),
            dma((9 * NZ,)),
            dma((9 * NZ,)),
            dma((16,)),
            dma((16,)),
            dma((19,)),
            dma((19,)),
        ],
        compiler_params=pltpu.CompilerParams(
            collective_id=0, has_side_effects=True, vmem_limit_bytes=56 * 2**20
        ),
        name="gcn_step",
    )(feats_t, adj_index.T, adj_weight.reshape(BLK * KB, TILE, TILE), weight, cotangent_t)
    return pl.pallas_call(
        keep,
        out_shape=shapes,
        name="results",
    )(*outs)


def solution(mesh):
    return jax.shard_map(
        body,
        mesh=mesh,
        in_specs=(P("cols", "rows"), P(), P("rows", None, None, None), P(), P("cols", "rows")),
        out_specs=(P("cols", "rows"), P("cols", None), P("cols", "rows")),
        check_vma=False,
    )
```

```python
import math

import jax
import jax.numpy as jnp
from jax import lax
from jax.experimental import pallas as pl
from jax.experimental.pallas import tpu as pltpu
from jax.sharding import PartitionSpec as P

MESH = pl.DeviceIdType.MESH
NZ, NY, NC, NX = 8, 4, 2, 4
BLK, KB, TILE, CAP, FR, UR = 16, 16, 128, 4, 32, 64
NODES_DEV = BLK * TILE
CH = 4
CN = NODES_DEV // CH
OWN = 64 * CAP
ZERO = BLK * KB
FWD_ORDER = (0, 7, 1, 6, 2, 5, 3, 4)
BWD_ORDER = (4, 3, 5, 2, 6, 1, 7, 0)
LAG = 3
WAT = (0, 2, 5)
F32, BF16 = jnp.float32, jnp.bfloat16
NT = (((1,), (1,)), ((), ()))


def group_sum(v, lane):
    n = v.shape[1]
    for step in (1, 2, 4, 8):
        up = pltpu.roll(v, n - step, 1)
        down = pltpu.roll(v, step, 1)
        v = v + jnp.where((lane & step) == 0, up, down)
    return v


def group_rank(named, lane):
    rank = jnp.zeros_like(named)
    for step in range(1, BLK):
        rank = rank + jnp.where((lane & (BLK - 1)) >= step, pltpu.roll(named, step, 1), 0)
    return rank


def send_tables(rows8, send_v, take_v, y, z, c, me):
    lane = lax.broadcasted_iota(jnp.int32, (8 * BLK, TILE), 1)
    target = (lane >> 4) * (8 * BLK) + (lane & 15) + (y * 2 + c) * BLK
    hit = jnp.zeros((8 * BLK, TILE), jnp.int32)
    for k in range(KB):
        hit = jnp.where(rows8[:, k:k + 1] == target, 1, hit)
    named = jnp.max(hit.reshape(8, BLK, TILE), axis=1)
    lane = lax.broadcasted_iota(jnp.int32, (8, TILE), 1)
    rank = group_rank(named, lane)
    for k in range(CAP):
        send_v[k * 8:(k + 1) * 8] = group_sum(jnp.where((named > 0) & (rank == k), lane & 15, 0), lane)
    d = lax.broadcasted_iota(jnp.int32, (8, TILE), 0)
    use = (named > 0) & ((d != me) | ((lane >> 4) != z))
    take_v[...] = jnp.where(use, d * CAP + jnp.minimum(rank, CAP - 1), 8 * CAP)


def slot_tables(rows8, slot_v, prev_v, last_v, r, me):
    own = rows8[pl.ds(pl.multiple_of(me * BLK, BLK), BLK)]
    lane = lax.broadcasted_iota(jnp.int32, (BLK, 64 * BLK), 1)
    hit = jnp.zeros((BLK, 64 * BLK), jnp.int32)
    for k in range(KB):
        hit = jnp.where(own[:, k:k + 1] == lane, 1, hit)
    lane8 = lax.broadcasted_iota(jnp.int32, (8, 64 * BLK), 1)
    named = jnp.broadcast_to(jnp.max(hit, axis=0, keepdims=True), (8, 64 * BLK))
    value = (lane8 >> 4) * CAP + jnp.minimum(group_rank(named, lane8), CAP - 1)
    value = jnp.where((lane8 >> 4) == r, OWN + (lane8 & 15), value)
    value = jnp.concatenate([value, value], axis=0)
    small = lax.broadcasted_iota(jnp.int32, (BLK, TILE), 1)
    e_lane = lax.broadcasted_iota(jnp.int32, (BLK, BLK * KB), 1)
    row = lax.broadcasted_iota(jnp.int32, (BLK, BLK * KB), 0)
    t_lane = lax.broadcasted_iota(jnp.int32, (BLK, 3 * TILE), 1)
    t_row = lax.broadcasted_iota(jnp.int32, (BLK, 3 * TILE), 0)
    slots = jnp.zeros((BLK, TILE), jnp.int32)
    spread = jnp.zeros((BLK, BLK * KB), jnp.int32)
    last = jnp.full((BLK, 3 * TILE), -1, jnp.int32)
    columns = []
    for k in range(KB):
        col = jnp.max(jnp.where(own[:, k:k + 1] == lane, value, 0), axis=1, keepdims=True)
        columns.append(col)
        slots = jnp.where(small == k, col, slots)
        spread = jnp.where((e_lane & 15) == k, col, spread)
        last = jnp.maximum(last, jnp.where(col == t_lane, t_row * KB + k, -1))
    slot_v[...] = slots
    by_lane = jnp.max(jnp.where((e_lane >> 4) == row, spread, 0), axis=0, keepdims=True)
    prev = jnp.zeros((BLK, TILE), jnp.int32)
    for k in range(KB):
        same = (columns[k] == by_lane) & (e_lane < row * KB + k)
        before = jnp.max(jnp.where(same, e_lane, -1), axis=1, keepdims=True)
        prev = jnp.where(small == k, before, prev)
    prev_v[...] = jnp.where(prev < 0, ZERO, prev)
    last = jnp.broadcast_to(jnp.max(last, axis=0, keepdims=True), (8, 3 * TILE))
    last_v[...] = jnp.where(last < 0, ZERO, last)


def kernel(
    feats_hbm, index_hbm, adj_hbm, weight_hbm, cot_hbm,
    out_hbm, wg_hbm, fg_hbm,
    feats, index, rows8, weight, cot, out, wg_out, fg_out,
    send_v, take_v, slot_v, prev_v, last_v, send_t, take_t, slot_t, prev_t, last_t,
    adj, zb, pk, panel, fwp, fwm, xg, gsend, grecv, gown, grad, pref, pk2, rb, fw2p, fw2m, zs_buf, zrp, zrm,
    wpart, wsib, wy, wz, wx, wt,
    lss, zss, zrs, yss, yrs, xss, xrs, gss, grs, yss2, yrs2, zss2, zrs2, wss, wrs,
):
    r = lax.axis_index("rows")
    x = lax.axis_index("cols")
    z, y, c = r // 8, (r // 2) % 4, r % 2
    me = y * 2 + c

    def dev(dz=0, dy=0, dc=0, dx=0):
        row = ((z + dz) % NZ) * 8 + ((y + dy) % NY) * 2 + (c + dc) % 2
        return {"rows": row, "cols": (x + dx) % NX}

    def rcopy(src, dst, ss, rs, **off):
        return pltpu.make_async_remote_copy(
            src_ref=src, dst_ref=dst, send_sem=ss, recv_sem=rs, device_id=dev(**off), device_id_type=MESH
        )

    def local(n, src, dst):
        cp = pltpu.make_async_copy(src, dst, lss.at[n])
        cp.start()
        return cp

    rows_copy = local(0, index_hbm.at[:, pl.ds(pl.multiple_of(z * 8 * BLK, 8 * BLK), 8 * BLK)], index)
    feats_copy = local(1, feats_hbm, feats)
    peers = [dict(dz=d) for d in range(1, 8)]
    peers += [dict(dy=a, dc=b) for a in range(4) for b in range(2) if (a or b) and (a, b) != (2, 1)]
    peers += [dict(dx=a, dc=b) for a in range(1, 4) for b in range(2)]
    barrier = pltpu.get_barrier_semaphore()
    for off in peers:
        pl.semaphore_signal(barrier, inc=1, device_id=dev(**off), device_id_type=MESH)

    weight_copy = local(2, weight_hbm, weight)
    cot_copy = local(3, cot_hbm, cot)
    adj_copy = local(4, adj_hbm, adj)
    rows_copy.wait()
    rows8[...] = index[...].T
    send_tables(rows8, send_v, take_v, y, z, c, me)
    send_copy = local(5, send_v, send_t)
    take_copy = local(6, take_v, take_t)
    feats_copy.wait()
    for b in range(BLK):
        blk = feats[:, b * TILE:(b + 1) * TILE]
        zb[0][b] = blk
        panel[OWN + b] = blk
    pl.semaphore_wait(barrier, len(peers))

    pending = []
    sent = {}
    done = set()

    half = BLK // 2
    whole = pl.ds(0, BLK)
    zcopies = {}

    def zsend(src, dst, direction, blocks):
        cp = rcopy(zb[src].at[blocks], zb[dst].at[blocks], zss.at[dst + 8 * (direction > 0)], zrs.at[dst + 8 * (direction > 0)], dz=direction)
        cp.start()
        zcopies.setdefault(dst, []).append(cp)
        pending.append(cp)

    def pack(dz, src, put, self_put):
        zs = (z + dz) % NZ

        def one(i, carry):
            dd = ((y + i // 2) % NY) * 2 + (c + i % 2) % 2
            src(i, dd, zs)
            return carry

        lax.fori_loop(0 if self_put else 1, 8, one, 0)

    def first_hops(dz, packs, fp, fm, ss, rs, copies):
        a = rcopy(packs.at[dz, 4], fp.at[dz], ss.at[dz * 9 + 7], rs.at[dz * 9 + 7], dy=1)
        b = rcopy(packs.at[dz, 5], fm.at[dz], ss.at[dz * 9 + 8], rs.at[dz * 9 + 8], dy=3)
        for cp in (a, b):
            cp.start()
            pending.append(cp)
        copies[dz] = ([], a, b)

    def ysends(dz, packs, dst_of, ss, rs, copies):
        list_, a, b = copies[dz]
        for n, (dy, dc) in enumerate(((1, 0), (1, 1), (3, 0), (3, 1), (0, 1))):
            cp = rcopy(packs.at[dz, dy * 2 + dc], dst_of(dz, y), ss.at[dz * 9 + n], rs.at[dz * 9 + n], dy=dy, dc=dc)
            cp.start()
            pending.append(cp)
            list_.append(cp)
        sent[dz] = (a, b, *list_)

    def drain(copies):
        for cp in copies:
            if id(cp) not in done:
                cp.wait_send()
                done.add(id(cp))

    def throttle(dz):
        drain(sent[dz])

    def forwards(dz, dst_of, fp, fm, ss, rs, copies):
        list_, a, b = copies[dz]
        a.wait_recv()
        f = rcopy(fp.at[dz], dst_of(dz, (y + 3) % NY), ss.at[dz * 9 + 5], rs.at[dz * 9 + 5], dy=1, dc=0)
        f.start()
        b.wait_recv()
        g = rcopy(fm.at[dz], dst_of(dz, (y + 1) % NY), ss.at[dz * 9 + 6], rs.at[dz * 9 + 6], dy=3, dc=1)
        g.start()
        pending.extend((f, g))
        list_ += [f, g]

    def panel_of(dz, yy):
        return panel.at[pl.ds((((z + dz) % NZ) * 8 + yy * 2 + c) * CAP, CAP)]

    ycopies = {}
    zsend(0, 7, 1, whole)
    zsend(0, 1, -1, whole)
    send_copy.wait()
    for at, dz in enumerate(FWD_ORDER):
        if dz:
            for cp in zcopies[dz]:
                cp.wait_recv()
            if dz in (7, 6):
                zsend(dz, dz - 1, 1, whole)
            elif dz == 5:
                zsend(5, 4, 1, pl.ds(0, half))
            elif dz in (1, 2):
                zsend(dz, dz + 1, -1, whole)
            elif dz == 3:
                zsend(3, 4, -1, pl.ds(half, half))

        def message(i, dd, zs, dz=dz):
            for k in range(CAP):
                pk[dz, i, k] = zb[dz][send_t[k * 8 + dd, zs * BLK]]

        pack(dz, message, None, False)
        if dz:
            zs = (z + dz) % NZ
            for k in range(CAP):
                panel[(zs * 8 + me) * CAP + k] = zb[dz][send_t[k * 8 + me, zs * BLK]]
        if at >= 2:
            throttle(FWD_ORDER[at - 2])
        first_hops(dz, pk, fwp, fwm, yss, yrs, ycopies)
        if at:
            forwards(FWD_ORDER[at - 1], panel_of, fwp, fwm, yss, yrs, ycopies)
        ysends(dz, pk, panel_of, yss, yrs, ycopies)
        if at == 0:
            slot_tables(rows8, slot_v, prev_v, last_v, r, me)
            table_copies = [local(7, slot_v, slot_t), local(8, prev_v, prev_t), local(9, last_v, last_t)]
        if at >= 3:
            for cp in ycopies[FWD_ORDER[at - 3]][0]:
                cp.wait_recv()
    forwards(FWD_ORDER[-1], panel_of, fwp, fwm, yss, yrs, ycopies)
    weight_copy.wait()
    w_all = jnp.concatenate(
        [weight[pl.ds(pl.multiple_of(((x + dx) % NX) * FR, FR), FR)] for dx in range(NX)], axis=0
    )
    unit = lax.broadcasted_iota(jnp.int32, (UR, NX * UR), 1) - lax.broadcasted_iota(jnp.int32, (UR, NX * UR), 0)
    pick = jnp.where(unit == x * UR, 1.0, 0.0).astype(BF16)
    w_rows = lax.dot_general(w_all, pick, NT, preferred_element_type=F32).astype(BF16)
    w_cols = lax.dot_general(pick, w_all, NT, preferred_element_type=F32).astype(BF16)
    for cp in (take_copy, *table_copies, cot_copy, adj_copy):
        cp.wait()
    for dz in FWD_ORDER[NZ - 3:]:
        for cp in ycopies[dz][0]:
            cp.wait_recv()

    xcopies = {}
    for q in range(CH):

        def block(n, carry, q=q):
            i = q * (BLK // CH) + n
            acc = jnp.zeros((TILE, FR), F32)
            for k in range(0, KB, 2):
                left = jnp.concatenate([adj[i * KB + k], adj[i * KB + k + 1]], axis=1)
                right = jnp.concatenate([panel[slot_t[i, k]], panel[slot_t[i, k + 1]]], axis=1)
                acc += lax.dot_general(left, right, NT, preferred_element_type=F32)
            xg[0, q, :, pl.ds(pl.multiple_of(n * TILE, TILE), TILE)] = acc.T.astype(BF16)
            return carry

        lax.fori_loop(0, BLK // CH, block, 0, unroll=True)
        for dx in (2, 1, 3):
            cp = rcopy(xg.at[0, q], xg.at[4 - dx, q], xss.at[q * 4 + dx], xrs.at[q * 4 + dx], dx=dx)
            cp.start()
            pending.append(cp)
            xcopies[q, dx] = cp

    gcopies = {}
    out_copies = []
    for q in range(CH):
        cols = pl.ds(q * CN, CN)
        for dx in (1, 3, 2):
            xcopies[q, dx].wait_recv()
        agg = xg[:, q].reshape(NX * FR, CN)
        pre = jnp.dot(w_cols, agg, preferred_element_type=F32)
        sig = jax.nn.sigmoid(pre)
        out[:, cols] = (pre * sig).astype(BF16)
        out_copies.append(local(10 + q, out.at[:, cols], out_hbm.at[:, cols]))
        pg = (cot[:, cols].astype(F32) * sig * (1.0 + pre * (1.0 - sig))).astype(BF16)
        part = jnp.dot(w_rows, pg, preferred_element_type=F32)
        gown[q] = part[0:FR]
        for dx in (2, 1, 3):
            gsend[dx, q] = part[dx * FR:(dx + 1) * FR].astype(BF16)
            cp = rcopy(gsend.at[dx, q], grecv.at[4 - dx, q], gss.at[q * 4 + dx], grs.at[q * 4 + dx], dx=dx)
            cp.start()
            pending.append(cp)
            gcopies[q, dx] = cp
        wg = lax.dot_general(pg, agg, NT, preferred_element_type=F32)
        if q == 0:
            wpart[...] = wg
        else:
            wpart[...] += wg

    hu = UR // 2
    w1 = rcopy(wpart.at[pl.ds(pl.multiple_of((1 - c) * hu, 8), hu)], wsib, wss.at[0], wrs.at[0], dc=1)
    w1.start()
    pending.append(w1)

    pref[ZERO] = jnp.zeros((FR, TILE), F32)

    def terms(i, carry):
        g = grad[i]
        for k in range(0, KB, 2):
            e = i * KB + k
            pair = jnp.concatenate([adj[e], adj[e + 1]], axis=1)
            term = jnp.dot(g, pair, preferred_element_type=F32)
            pref[e] = term[:, :TILE] + pref[prev_t[i, k]]
            pref[e + 1] = term[:, TILE:] + pref[prev_t[i, k + 1]]
        return carry

    nb = BLK // CH
    for q in range(CH):
        for dx in (1, 3, 2):
            gcopies[q, dx].wait_recv()
        g = gown[q] + grecv[1, q].astype(F32) + grecv[2, q].astype(F32) + grecv[3, q].astype(F32)
        g = g.astype(BF16)
        for n in range(nb):
            grad[q * nb + n] = g[:, n * TILE:(n + 1) * TILE]
        lax.fori_loop(q * nb, (q + 1) * nb, terms, 0, unroll=True)

    def weight_y():
        w1.wait_recv()
        wy[y] = wpart[pl.ds(pl.multiple_of(c * hu, 8), hu)] + wsib[...]
        copies = []
        for dy in (1, 2, 3):
            cp = rcopy(wy.at[y], wy.at[y], wss.at[dy], wrs.at[dy], dy=dy)
            cp.start()
            pending.append(cp)
            copies.append(cp)
        return copies

    def weight_z():
        for cp in w2:
            cp.wait_recv()
        wz[z] = (wy[0] + wy[1]) + (wy[2] + wy[3])
        copies = []
        for dz in range(1, NZ):
            cp = rcopy(wz.at[z], wz.at[z], wss.at[3 + dz], wrs.at[3 + dz], dz=dz)
            cp.start()
            pending.append(cp)
            copies.append(cp)
        return copies

    ycopies2 = {}

    def rb_of(dz, yy):
        return rb[dz].at[pl.ds((yy * 2 + c) * CAP, CAP)]

    for dz in range(NZ):
        rb[dz][8 * CAP] = jnp.zeros((FR, TILE), BF16)
    zin = {}

    def reduce_chunk(dz):
        for cp in ycopies2[dz][0]:
            cp.wait_recv()
        zs = (z + dz) % NZ
        for h in ((1, 0) if dz == 3 else (0, 1)):
            arrived = []
            for cp, buf in zin.get((dz, h), ()):
                cp.wait_recv()
                arrived.append(buf)

            def total(n, carry, h=h, arrived=tuple(arrived)):
                b = h * half + n
                acc = jnp.zeros((FR, TILE), F32)
                for d in range(8):
                    acc += rb[dz][take_t[d, zs * BLK + b]].astype(F32)
                for buf in arrived:
                    acc += buf[dz, b].astype(F32)
                if dz:
                    zs_buf[dz, b] = acc.astype(BF16)
                else:
                    acc += pref[last_t[0, OWN + b]]
                    fg_out[:, pl.ds(pl.multiple_of(b * TILE, TILE), TILE)] = acc
                return carry

            lax.fori_loop(0, half, total, 0)
            if not dz:
                cols = pl.ds(h * half * TILE, half * TILE)
                out_copies.append(local(15 if h else 9, fg_out.at[:, cols], fg_hbm.at[:, cols]))
            if dz:
                up = dz < 4 or (dz == 4 and h == 0)
                to = dz - 1 if up else (dz + 1) % NZ
                buf = zrp if up else zrm
                blocks = pl.ds(h * half, half)
                n = dz * 2 + h
                cp = rcopy(zs_buf.at[dz, blocks], buf.at[to, blocks], zss2.at[n], zrs2.at[n], dz=1 if up else -1)
                cp.start()
                pending.append(cp)
                zin.setdefault((to, h), []).append((cp, buf))

    def weight_cols():
        for cp in w3:
            cp.wait_recv()
        wx[0, c] = (((wz[0] + wz[1]) + (wz[2] + wz[3])) + ((wz[4] + wz[5]) + (wz[6] + wz[7]))) * (
            1.0 / math.sqrt(NODES_DEV * 64)
        )
        w4 = []
        for dx in range(4):
            for dc in range(2):
                if dx or dc:
                    n = 11 + dx * 2 + dc
                    cp = rcopy(wx.at[0, c], wx.at[(4 - dx) % 4, c], wss.at[n], wrs.at[n], dx=dx, dc=dc)
                    cp.start()
                    pending.append(cp)
                    w4.append(cp)
        return w4

    sent.clear()
    old = len(pending)
    marks = []
    for at, dz in enumerate(BWD_ORDER):

        def term(i, dd, zs, dz=dz):
            for k in range(CAP):
                pk2[dz, i, k] = pref[last_t[0, (zs * 8 + dd) * CAP + k]].astype(BF16)

        pack(dz, term, None, False)
        zs = (z + dz) % NZ
        for k in range(CAP):
            if dz:
                rb[dz][me * CAP + k] = pref[last_t[0, (zs * 8 + me) * CAP + k]].astype(BF16)
            else:
                rb[dz][me * CAP + k] = jnp.zeros((FR, TILE), BF16)
        if at >= 2:
            throttle(BWD_ORDER[at - 2])
        first_hops(dz, pk2, fw2p, fw2m, yss2, yrs2, ycopies2)
        if at:
            forwards(BWD_ORDER[at - 1], rb_of, fw2p, fw2m, yss2, yrs2, ycopies2)
        ysends(dz, pk2, rb_of, yss2, yrs2, ycopies2)
        if at == WAT[0]:
            w2 = weight_y()
        if at == WAT[1]:
            w3 = weight_z()
        if at == WAT[2]:
            w4 = weight_cols()
        if at >= LAG:
            reduce_chunk(BWD_ORDER[at - LAG])
        marks.append(len(pending))
        if at < 4:
            drain(pending[old * at // 4:old * (at + 1) // 4])
        else:
            drain(pending[marks[at - 4]:marks[at - 3]])
    forwards(0, rb_of, fw2p, fw2m, yss2, yrs2, ycopies2)
    drain(pending[old:marks[-3]])
    for dz in BWD_ORDER[NZ - LAG:-1]:
        reduce_chunk(dz)

    for cp in w4:
        cp.wait_recv()
    for dx in range(4):
        for cc in range(2):
            f0 = ((4 - dx) % 4) * FR
            row = pl.multiple_of(((x + dx) % NX) * UR + cc * hu, 8)
            wt[pl.ds(row, hu), 0:FR] = wx[dx, cc][:, f0:f0 + FR]
    wg_out[...] = wt[...].T[0:FR]
    out_copies.append(local(14, wg_out, wg_hbm))
    drain(pending[:-4])
    reduce_chunk(0)
    for cp in out_copies:
        cp.wait()

    drain(pending)


def keep(a, b, c, a_out, b_out, c_out):
    a_out[...] = a[...]
    b_out[...] = b[...]
    c_out[...] = c[...]


def body(feats_t, adj_index, adj_weight, weight, cotangent_t):
    hbm = pl.BlockSpec(memory_space=pl.ANY)
    dma = pltpu.SemaphoreType.DMA
    blk = (FR, TILE)
    V = pltpu.VMEM
    table = lambda space: [space(s, jnp.int32) for s in ((4 * 8, TILE), (8, TILE), (BLK, TILE), (BLK, TILE), (8, 3 * TILE))]
    shapes = (
        jax.ShapeDtypeStruct((UR, NODES_DEV), BF16),
        jax.ShapeDtypeStruct((FR, NX * UR), F32),
        jax.ShapeDtypeStruct((FR, NODES_DEV), F32),
    )
    outs = pl.pallas_call(
        kernel,
        out_shape=shapes,
        in_specs=[hbm] * 5,
        out_specs=(hbm,) * 3,
        scratch_shapes=[
            V((FR, NODES_DEV), BF16),
            V((KB, 8 * BLK), jnp.int32),
            V((8 * BLK, KB), jnp.int32),
            V((NX * FR, NX * UR), BF16),
            V((UR, NODES_DEV), BF16),
            V((UR, NODES_DEV), BF16),
            V((FR, NX * UR), F32),
            V((FR, NODES_DEV), F32),
            *table(V),
            *table(pltpu.SMEM),
            V((BLK * KB, TILE, TILE), BF16),
            [V((BLK, *blk), BF16) for _ in range(NZ)],
            V((NZ, 8, CAP, *blk), BF16),
            V((OWN + BLK, *blk), BF16),
            V((NZ, CAP, *blk), BF16),
            V((NZ, CAP, *blk), BF16),
            V((NX, CH, FR, CN), BF16),
            V((NX, CH, FR, CN), BF16),
            V((NX, CH, FR, CN), BF16),
            V((CH, FR, CN), F32),
            V((BLK, *blk), BF16),
            V((BLK * KB + 1, *blk), F32),
            V((NZ, 8, CAP, *blk), BF16),
            [V((8 * CAP + 1, *blk), BF16) for _ in range(NZ)],
            V((NZ, CAP, *blk), BF16),
            V((NZ, CAP, *blk), BF16),
            V((NZ, BLK, *blk), BF16),
            V((NZ, BLK, *blk), BF16),
            V((NZ, BLK, *blk), BF16),
            V((UR, NX * FR), F32),
            V((UR // 2, NX * FR), F32),
            V((NY, UR // 2, NX * FR), F32),
            V((NZ, UR // 2, NX * FR), F32),
            V((NX, NC, UR // 2, NX * FR), F32),
            V((NX * UR, TILE), F32),
            dma((16,)),
            dma((16,)),
            dma((16,)),
            dma((9 * NZ,)),
            dma((9 * NZ,)),
            dma((16,)),
            dma((16,)),
            dma((16,)),
            dma((16,)),
            dma((9 * NZ,)),
            dma((9 * NZ,)),
            dma((16,)),
            dma((16,)),
            dma((19,)),
            dma((19,)),
        ],
        compiler_params=pltpu.CompilerParams(
            collective_id=0, has_side_effects=True, vmem_limit_bytes=56 * 2**20
        ),
        name="gcn_step",
    )(feats_t, adj_index.T, adj_weight.reshape(BLK * KB, TILE, TILE), weight, cotangent_t)
    return pl.pallas_call(
        keep,
        out_shape=shapes,
        name="results",
    )(*outs)


def solution(mesh):
    return jax.shard_map(
        body,
        mesh=mesh,
        in_specs=(P("cols", "rows"), P(), P("rows", None, None, None), P(), P("cols", "rows")),
        out_specs=(P("cols", "rows"), P("cols", None), P("cols", "rows")),
        check_vma=False,
    )
```
